32 devices in a mesh: seq: 8 (over z, x), head: 4 (over y, core).
Axes of the slice: x: 2, y: 2, z: 4, core: 2. Of those that a mesh axis runs over, the one named last changes fastest.
Arguments:
- x_points: bfloat16 [16384, 512], P('seq', 'head'), may hold values from -6 to 6
- hilbert_index: int32 [16384], P('seq'), may hold values from 0 to 16383, as said below
- w_qkv: bfloat16 [2, 512, 3, 512], P(None, None, None, 'head'), may hold values from -3 to 3
- w_out: bfloat16 [2, 512, 512], P(None, 'head'), may hold values from -0.25 to 0.25
- w_up: bfloat16 [2, 2048, 512], P(None, 'head'), may hold values from -0.25 to 0.25
- w_down: bfloat16 [2, 2048, 512], P(None, 'head'), may hold values from -0.125 to 0.125
Outputs:
- z_out: bfloat16 [16384, 512], P('seq', 'head')
The draws below stay inside these ranges and needn't reach their ends.
Inputs may be any that keep to these rules, and one draw needn't show every extreme that they name: `hilbert_index`: A permutation of all point positions. Call rows k * 2048 to (k + 1) * 2048 - 1 of either order shard k; the first and the last shard count as next to each other. Of the points of Z-order shard k, at most 1376 have a Hilbert position in shard k, at most 384 in each of the shards k - 1 and k + 1, and exactly 32 in every other shard. Some shard keeps exactly 1376, and some pair of neighbouring shards reaches 384 in both directions.
All inputs are finite; a program needn't handle non-finite values.
Results may differ from the reference program's by a relative error of at most 0.025.
Values may be sent and summed in bfloat16 or wider, within the bound.
A program may use at most 64 MiB of HBM per device.

```python
import jax
import jax.numpy as jnp
from jax import lax

D = 512
HEADS = 16
HEAD_DIM = 32
FF = 2048
PATCH = 1024
LAYERS = 2
PTS_DEV = 2048
NPTS = 16384
N_SEQ = 8


def draw_hilbert_index(key, part):
    shards = N_SEQ
    points = PTS_DEV
    near = points // 8
    far = points // (8 * shards)
    bump_most = points // 16
    own = points - 2 * near - (shards - 3) * far
    key_v, key_r, key_src, key_dst = jax.random.split(jax.random.fold_in(key, 17), 4)
    ids = jnp.arange(shards)
    gap = (ids[None, :] - ids[:, None]) % shards
    counts = jnp.where(gap == 0, own, jnp.where((gap == 1) | (gap == shards - 1), near, far)).astype(jnp.int32)
    bumps = jax.random.randint(key_v, (shards,), 0, bump_most + 1)
    start = jax.random.randint(key_r, (), 0, shards)
    bumps = bumps.at[(start - 1) % shards].set(0)
    bumps = bumps.at[start].set(0)
    bumps = bumps.at[(start + 2) % shards].set(bump_most)
    following = (ids + 1) % shards
    counts = counts.at[ids, ids].add(-bumps)
    counts = counts.at[following, following].add(-bumps)
    counts = counts.at[ids, following].add(bumps)
    counts = counts.at[following, ids].add(bumps)
    upper = jnp.cumsum(counts, axis=1)
    lower = upper - counts
    recv_start = jnp.cumsum(counts, axis=0) - counts
    ranks = jnp.arange(points)
    target = jnp.sum((ranks[None, :, None] >= upper[:, None, :]).astype(jnp.int32), axis=2)
    within = ranks[None, :] - jnp.take_along_axis(lower, target, axis=1)
    arrive = jnp.take_along_axis(recv_start, target, axis=1) + within
    src_perm = jax.vmap(lambda sub: jax.random.permutation(sub, points))(jax.random.split(key_src, shards))
    dst_perm = jax.vmap(lambda sub: jax.random.permutation(sub, points))(jax.random.split(key_dst, shards))
    position = target * points + dst_perm[target, arrive]
    result = jnp.zeros((shards, points), jnp.int32).at[ids[:, None], src_perm].set(position.astype(jnp.int32))
    return result.reshape(shards * points)


def draw_w_qkv(key, part):
    key_base = jax.random.fold_in(jax.random.fold_in(key, 29), 0)
    base = jax.random.truncated_normal(key_base, -4.0, 4.0, (LAYERS, D, 3, D), jnp.float32)
    query_cols = base[:, :, 0] * 2.0
    key_cols = base[:, :, 1] * 2.0
    value_cols = base[:, :, 2]
    stacked = jnp.stack([query_cols, key_cols, value_cols], axis=2) / jnp.sqrt(jnp.float32(D))
    return stacked.astype(jnp.bfloat16)


def levels(own_key, extent, cuts, smallest, high):
    level, own = 1.0, jax.random.fold_in(own_key, 6)
    for dim, shards_of in cuts:
        steps = jnp.exp(jax.random.uniform(jax.random.fold_in(own, dim), (shards_of,), jnp.float32, smallest / len(cuts), high / len(cuts)))
        level = level * jnp.repeat(steps, extent[dim] // shards_of).reshape([-1 if axis == dim else 1 for axis in range(len(extent))])
    return level


def noise(own_key, shape, width, bound, cuts=(), dtype=jnp.bfloat16):
    drawn = jax.random.normal(own_key, shape, jnp.float32) * width
    if len(cuts) > 0:
        drawn = levels(own_key, shape, cuts, -0.22, 0.18) * drawn
    return jnp.clip(drawn, min=-bound, max=bound).astype(dtype)


def setup_inputs(seed: int = 0) -> dict:
    arg_keys = jax.random.split(jax.random.key(seed), 7)
    x_points = noise(arg_keys[0], (NPTS, D), 1.0, 6.0, ((0, 8), (1, 4)))
    hilbert_index = draw_hilbert_index(jax.random.fold_in(arg_keys[6], 71), 0)
    w_qkv = draw_w_qkv(jax.random.fold_in(arg_keys[6], 71), 0)
    w_out = noise(arg_keys[3], (LAYERS, D, D), D ** -0.5, 0.25, ((1, 4),))
    w_up = noise(arg_keys[4], (LAYERS, FF, D), D ** -0.5, 0.25, ((1, 4),))
    w_down = noise(arg_keys[5], (LAYERS, FF, D), FF ** -0.5, 0.125, ((1, 4),))
    return dict(x_points=x_points, hilbert_index=hilbert_index, w_qkv=w_qkv, w_out=w_out, w_up=w_up, w_down=w_down)


EPS = 1e-05

def layer_norm(rows):
    values = rows.astype(jnp.float32)
    center = values - lax.optimization_barrier(jnp.mean(values, axis=-1, keepdims=True))
    spread = lax.optimization_barrier(jnp.mean(center * center, axis=-1, keepdims=True))
    return (center * lax.rsqrt(spread + EPS)).astype(jnp.bfloat16)

def attend(normed, wqkv):
    total = normed.shape[0]
    packed = jnp.dot(normed, wqkv.reshape(D, 3 * D), preferred_element_type=jnp.float32).astype(jnp.bfloat16)
    packed = packed.reshape(total // PATCH, PATCH, 3, HEADS, HEAD_DIM)

    def one_patch(block):
        query_rows = block[:, 0].astype(jnp.float32)
        key_rows = block[:, 1].astype(jnp.float32)
        value_rows = block[:, 2].astype(jnp.float32)
        scores = jnp.einsum('qhd,khd->hqk', query_rows, key_rows) * HEAD_DIM ** (-0.5)
        weights = jax.nn.softmax(scores, axis=-1).astype(jnp.bfloat16)
        mixed = jnp.einsum('hqk,khd->qhd', weights.astype(jnp.float32), value_rows)
        return mixed.astype(jnp.bfloat16).reshape(PATCH, D)
    return lax.map(one_patch, packed).reshape(total, D)

def run_layer(hidden, wqkv, wout, wup, wdown):
    normed = layer_norm(hidden)
    attended = attend(normed, wqkv)
    mid = (hidden.astype(jnp.float32) + jnp.dot(attended, wout, preferred_element_type=jnp.float32)).astype(jnp.bfloat16)
    mid_norm = layer_norm(mid)
    inner = jax.nn.gelu(jnp.dot(mid_norm, wup.T, preferred_element_type=jnp.float32), approximate=False).astype(jnp.bfloat16)
    return (mid.astype(jnp.float32) + jnp.dot(inner, wdown, preferred_element_type=jnp.float32)).astype(jnp.bfloat16)

def reference(x_points, hilbert_index, w_qkv, w_out, w_up, w_down):
    first = run_layer(x_points, w_qkv[0], w_out[0], w_up[0], w_down[0])
    hilbert_rows = jnp.zeros_like(first).at[hilbert_index].set(first)
    second = run_layer(hilbert_rows, w_qkv[1], w_out[1], w_up[1], w_down[1])
    return second[hilbert_index]
```

```python
import functools
import math

import jax
import jax.numpy as jnp
from jax import lax
from jax.experimental import pallas as pl
from jax.experimental.pallas import tpu as pltpu
from jax.sharding import PartitionSpec as P

HEAD_DIM = 32
PATCH = 1024
EPS = 1e-05
LANES = 128
BASE = 64
MESH = pl.DeviceIdType.MESH
F32 = jnp.float32
BF16 = jnp.bfloat16


def block(index, size):
    return pl.ds(pl.multiple_of(index * size, size), size)


def norm(values):
    center = values - jnp.mean(values, axis=-1, keepdims=True)
    spread = jnp.mean(center * center, axis=-1, keepdims=True)
    return (center * lax.rsqrt(spread + EPS)).astype(BF16)


def matmul(a, b):
    return jnp.dot(a, b, preferred_element_type=F32)


def matmul_nt(a, b):
    return lax.dot_general(a, b, (((1,), (1,)), ((), ())), preferred_element_type=F32)


def gelu(x):
    return 0.5 * x * (1.0 + lax.erf(x * math.sqrt(0.5)))


def chosen_rows(count, base, index_row):
    slots = lax.broadcasted_iota(jnp.int32, (count, index_row.shape[1]), 0) + base
    return (slots == index_row).astype(F32).astype(BF16)


def chosen_cols(index_col, count):
    slots = lax.broadcasted_iota(jnp.int32, (index_col.shape[0], count), 1)
    return (slots == index_col).astype(F32).astype(BF16)


QKV, OUT, UP, DOWN = 2, 3, 4, 5


def program_kernel(
    n_head, peers, near, cap,
    x_ref, wqkv_ref, wout_ref, wup_ref, wdown_ref, index_ref,
    final_ref,
    rows, wqkv, wout, wup, wdown, normed, q, k, v, attended, mid_norm, result, cols, moved,
    pick, keep, spread, near_out, far_out, near_in, far_in, got, codes, partial, code_ref,
    local_sem, send_sem, recv_sem, out_send, out_recv, seq_send, seq_recv,
):
    me = lax.axis_index("head")
    seq = lax.axis_index("seq")
    side = lax.rem(seq, 2)
    neighbour = seq + 1 - 2 * side
    sibling = me + 1 - 2 * lax.rem(me, 2)
    partner = lax.rem(me + n_head // 2, n_head)
    half = lax.rem(me, 2)
    own_rows, width = result.shape
    points = moved.shape[0]
    slots = 2 * near + peers * cap
    chunk = PATCH // 2

    barrier = pltpu.get_barrier_semaphore()
    for step in range(1, n_head):
        to = lax.rem(me + step, n_head)
        pl.semaphore_signal(barrier, inc=1, device_id={"head": to}, device_id_type=MESH)
    for step in range(1, peers):
        to = lax.rem(seq + step, peers)
        pl.semaphore_signal(barrier, inc=1, device_id={"seq": to}, device_id_type=MESH)
    pl.semaphore_wait(barrier, n_head + peers - 2)

    def source(l, i, to):
        if i < 2:
            start = pl.multiple_of((to // 2) * PATCH + i * chunk, chunk)
            return (x_ref if l == 0 else moved).at[pl.ds(start, chunk)]
        return (wqkv_ref, wout_ref, wup_ref, wdown_ref)[i - QKV].at[l]

    def place(l, i, owner):
        if i < 2:
            return rows.at[l, pl.ds(i * chunk, chunk), block(owner, LANES)]
        if i == QKV:
            return wqkv.at[l, owner // 2, :, :, block(lax.rem(owner, 2), LANES)]
        ref = (wout, wup, wdown)[i - OUT]
        return ref.at[l, block(owner, ref.shape[1] // n_head)]

    def part(i, ref, which):
        if i < 2:
            return ref
        if i == QKV:
            return ref.at[:, block(which, ref.shape[1] // 2)]
        return ref.at[block(which, ref.shape[0] // 2)]

    def own(l, i):
        return pltpu.make_async_copy(source(l, i, me), place(l, i, me), local_sem.at[l, i])

    def remote(l, i, way, src, dst, device):
        return pltpu.make_async_remote_copy(
            src_ref=src,
            dst_ref=dst,
            send_sem=send_sem.at[l, i, way],
            recv_sem=recv_sem.at[l, i, way],
            device_id=device,
            device_id_type=MESH,
        )

    def to_partner(l, i):
        src = part(i, source(l, i, partner), side)
        return remote(l, i, 0, src, part(i, place(l, i, me), side), {"head": partner})

    def to_sibling(l, i):
        return remote(l, i, 1, source(l, i, sibling), place(l, i, me), {"head": sibling})

    def forward(l, i):
        ref = part(i, place(l, i, partner), side)
        return remote(l, i, 2, ref, ref, {"head": sibling})

    def to_neighbour(l, i):
        ref = part(i, place(l, i, partner), side)
        return remote(l, i, 3, ref, ref, {"seq": neighbour})

    def forward_other(l, i):
        ref = part(i, place(l, i, partner), 1 - side)
        return remote(l, i, 4, ref, ref, {"head": sibling})

    def send(l, i):
        to_partner(l, i).start()
        own(l, i).start()

    def relay(l, i):
        to_partner(l, i).wait_recv()
        if i >= QKV:
            to_neighbour(l, i).start()
        forward(l, i).start()

    def relay_other(l, i):
        to_neighbour(l, i).wait_recv()
        forward_other(l, i).start()

    def ready(l, i):
        own(l, i).wait()
        to_sibling(l, i).wait_recv()
        forward(l, i).wait_recv()
        if i >= QKV:
            forward_other(l, i).wait_recv()

    def seq_copy(turn, step):
        to = lax.rem(seq + step, peers)
        back = turn == 2
        if step == 1:
            at = pl.ds(near if back else 0, near)
            src, dst = near_out.at[turn, at], near_in.at[turn, at]
        elif step == peers - 1:
            at = pl.ds(0 if back else near, near)
            src, dst = near_out.at[turn, at], near_in.at[turn, at]
        else:
            src, dst = far_out.at[turn, to], far_in.at[turn, seq]
        return pltpu.make_async_remote_copy(
            src_ref=src,
            dst_ref=dst,
            send_sem=seq_send.at[turn, step],
            recv_sem=seq_recv.at[turn, step],
            device_id={"seq": to},
            device_id_type=MESH,
        )

    def seq_send_rows(turn, table):
        for lo in range(0, 2 * near, near):
            near_out[turn, lo : lo + near] = matmul(pick[lo : lo + near], table).astype(BF16)
            seq_copy(turn, (1 if lo == 0 else peers - 1) if turn != 2 else (peers - 1 if lo == 0 else 1)).start()
        packed = matmul(pick[2 * near :], table)
        for peer in range(peers):
            far_out[turn, peer] = packed[peer * cap : (peer + 1) * cap].astype(BF16)
        for step in range(2, peers - 1):
            seq_copy(turn, step).start()

    def seq_receive(turn):
        for step in range(1, peers):
            seq_copy(turn, step).wait_recv()
        for step in (0, 1, peers - 1):
            unused = lax.rem(seq + step, peers)
            far_in[turn, unused] = jnp.zeros(far_in.shape[2:], BF16)
        got[: 2 * near] = near_in[turn]
        for peer in range(peers):
            at = 2 * near + peer * cap
            got[at : at + cap] = far_in[turn, peer].astype(F32).astype(BF16)

    def normalise(l, i):
        @pl.loop(0, chunk // LANES)
        def _(j):
            at = pl.ds(pl.multiple_of(i * chunk + j * LANES, LANES), LANES)
            normed[at] = norm(rows[l, at].astype(F32))

    def keys_values(l, chip, i):
        at = pl.ds(i * chunk, chunk)
        keys = matmul(normed[at], wqkv[l, chip, 1]).astype(BF16)
        values = matmul(normed[at], wqkv[l, chip, 2]).astype(BF16)
        for part_of in range(2):
            cut = slice(part_of * LANES, (part_of + 1) * LANES)
            k[chip * 2 + part_of, at] = keys[:, cut]
            v[chip * 2 + part_of, at, :LANES] = values[:, cut]

    def queries(l, chip):
        scale = HEAD_DIM ** (-0.5) * math.log2(math.e)
        mine = pl.ds(pl.multiple_of(half * own_rows, own_rows), own_rows)
        found = (matmul(normed[mine], wqkv[l, chip, 0]) * scale).astype(BF16)
        for part_of in range(2):
            q[chip * 2 + part_of] = found[:, part_of * LANES : (part_of + 1) * LANES]

    def attend(chip, first, last):
        owner = lax.broadcasted_iota(jnp.int32, (256, LANES), 1) // HEAD_DIM

        @pl.loop(first, last)
        def _(step):
            group = chip * 2 + step // 2
            at = block(lax.rem(step, 2), 256)
            query = q[group, at]
            total = jnp.zeros((256, LANES), F32)
            norms = jnp.ones((256, LANES), F32)
            for head in range(LANES // HEAD_DIM):
                chosen = owner == head
                scores = matmul_nt(jnp.where(chosen, query, jnp.zeros_like(query)), k[group])
                top = jnp.max(scores, axis=-1, keepdims=True)
                weights = jnp.exp2(scores - top).astype(BF16)
                mixed = matmul(weights, v[group])
                total = jnp.where(chosen, mixed[:, :LANES], total)
                norms = jnp.where(chosen, mixed[:, LANES:], norms)
            attended[at, block(group, LANES)] = (total / norms).astype(BF16)

    def out_copy(l, piece, step):
        to = lax.rem(me + step, n_head)
        at = pl.ds(pl.multiple_of(me * own_rows + piece * 256, 256), 256)
        return pltpu.make_async_remote_copy(
            src_ref=result.at[block(piece, 256), block(to, LANES)],
            dst_ref=cols.at[l, at],
            send_sem=out_send.at[l, piece, step],
            recv_sem=out_recv.at[l, piece, step],
            device_id={"head": to},
            device_id_type=MESH,
        )

    hidden = wup.shape[1]
    hidden_cols = 512

    def feed_forward(l):
        for piece in range(own_rows // 256):
            at = pl.ds(piece * 256, 256)
            mine = pl.ds(pl.multiple_of(half * own_rows + piece * 256, 256), 256)
            summed = (rows[l, mine].astype(F32) + matmul(attended[at], wout[l])).astype(BF16)
            total = summed.astype(F32)
            mid_norm[at] = norm(total)
            partial[...] = total

            @pl.loop(0, hidden // hidden_cols)
            def _(j):
                hid = block(j, hidden_cols)
                inner = gelu(matmul_nt(mid_norm[at], wup[l, hid])).astype(BF16)
                partial[...] += matmul(inner, wdown[l, hid])

            result[at] = partial[...].astype(BF16)
            for step in range(2, n_head):
                out_copy(l, piece, step).start()
            out_copy(l, piece, 1).start()
            cols[l, pl.ds(pl.multiple_of(me * own_rows + piece * 256, 256), 256)] = result[
                at, block(me, LANES)
            ]

    def out_wait(l):
        for piece in range(own_rows // 256):
            for step in range(1, n_head):
                out_copy(l, piece, step).wait()

    for i in range(6):
        send(0, i)
        if i < 3:
            to_sibling(0, i).start()
    send(1, QKV)
    send(1, OUT)

    where_to = index_ref[...]
    bounds = lax.broadcasted_iota(jnp.int32, (peers, points), 0) * points
    hot = jnp.where((where_to >= bounds) & (where_to < bounds + points), 1.0, 0.0)
    lower = lax.broadcasted_iota(jnp.int32, (LANES, LANES), 0)
    upper = lax.broadcasted_iota(jnp.int32, (LANES, LANES), 1)
    triangle = jnp.where(lower <= upper, 1.0, 0.0).astype(BF16)
    carried = jnp.zeros((peers, 1), F32)
    counts = []
    for at in range(0, points, LANES):
        piece = hot[:, at : at + LANES]
        counts.append(matmul(piece.astype(BF16), triangle) + carried)
        carried = carried + jnp.sum(piece, axis=1, keepdims=True)
    rank = jnp.sum(jnp.concatenate(counts, axis=1) * hot, axis=0, keepdims=True)
    rank = rank.astype(jnp.int32) - 1
    device_start = jnp.sum(hot * bounds.astype(F32), axis=0, keepdims=True).astype(jnp.int32)
    order = lax.broadcasted_iota(jnp.int32, (peers, points), 0).astype(F32)
    device = jnp.sum(hot * order, axis=0, keepdims=True).astype(jnp.int32)
    row = where_to - device_start
    following = lax.rem(seq + 1, peers)
    previous = lax.rem(seq + peers - 1, peers)
    slot = jnp.where(device == previous, near + rank, 2 * near + device * cap + rank)
    slot = jnp.where(device == following, rank, slot)
    slot = jnp.where(device == seq, -1, slot)
    kept = jnp.where(device == seq, row, -1)
    coded = row + BASE
    high = lax.shift_right_logical(coded, jnp.full_like(coded, BASE.bit_length() - 1))
    low = coded - high * BASE
    lane = lax.broadcasted_iota(jnp.int32, (LANES, points), 0)
    fields = jnp.where(lane == 2, slot, jnp.where(lane == 3, kept, 0))
    fields = jnp.where(lane == 0, high, jnp.where(lane == 1, low, fields))
    code_ref[...] = jnp.transpose(fields.astype(F32), (1, 0))

    @pl.loop(0, slots // LANES)
    def _(i):
        pick[block(i, LANES)] = chosen_rows(LANES, i * LANES, slot)

    relay(0, 0)
    seq_send_rows(0, code_ref[...].astype(BF16))
    relay(0, 1)
    for group in range(n_head):
        v[group, :, LANES:] = jnp.ones((PATCH, LANES), BF16)
    mine_chip = me // 2
    other_chip = partner // 2
    own(0, QKV).wait()
    to_sibling(0, QKV).wait_recv()
    ready(0, 0)
    normalise(0, 0)
    keys_values(0, mine_chip, 0)
    ready(0, 1)
    normalise(0, 1)
    keys_values(0, mine_chip, 1)
    queries(0, mine_chip)
    relay(0, QKV)
    to_sibling(0, OUT).start()
    seq_receive(0)
    codes[...] = got[...].astype(F32)
    turned = jnp.transpose(codes[...], (1, 0))
    target = (turned[0:1] * BASE + turned[1:2]).astype(jnp.int32) - BASE

    @pl.loop(0, points // LANES)
    def _(i):
        spread[block(i, LANES)] = chosen_rows(LANES, i * LANES, target)

    attend(mine_chip, 0, 2)
    relay(0, OUT)
    to_sibling(0, UP).start()
    attend(mine_chip, 2, 3)
    relay_other(0, QKV)
    to_sibling(0, DOWN).start()
    attend(mine_chip, 3, 4)
    relay_other(0, OUT)

    @pl.loop(0, points // LANES)
    def _(i):
        keep[block(i, LANES)] = chosen_rows(LANES, i * LANES, kept)

    forward(0, QKV).wait_recv()
    forward_other(0, QKV).wait_recv()
    for i in range(2):
        keys_values(0, other_chip, i)
    queries(0, other_chip)
    relay(0, UP)
    attend(other_chip, 0, 2)
    relay_other(0, UP)
    relay(0, DOWN)
    attend(other_chip, 2, 4)
    relay_other(0, DOWN)
    to_sibling(1, QKV).start()
    to_sibling(1, OUT).start()
    relay(1, QKV)
    ready(0, OUT)
    ready(0, UP)
    ready(0, DOWN)
    feed_forward(0)
    send(1, UP)
    to_sibling(1, UP).start()
    relay_other(1, QKV)
    relay(1, OUT)
    out_wait(0)

    seq_send_rows(1, cols[0])
    relay_other(1, OUT)
    moved[...] = matmul(keep[...], cols[0]).astype(BF16)
    seq_receive(1)
    moved[...] = (moved[...].astype(F32) + matmul(spread[...], got[...])).astype(BF16)

    for i in (0, 1, DOWN):
        send(1, i)
        to_sibling(1, i).start()

    @pl.loop(0, slots // LANES)
    def _(i):
        at = block(i, LANES)
        both = codes[at]
        place_col = (both[:, 0:1] * BASE + both[:, 1:2]).astype(jnp.int32) - BASE
        pick[at] = chosen_cols(place_col, points)

    relay(1, UP)
    relay(1, 0)
    relay(1, 1)
    ready(1, 0)
    normalise(1, 0)
    ready(1, QKV)
    for chip in range(n_head // 2):
        keys_values(1, chip, 0)
    ready(1, 1)
    normalise(1, 1)
    for chip in range(n_head // 2):
        keys_values(1, chip, 1)
    for chip in range(n_head // 2):
        queries(1, chip)
    relay_other(1, UP)
    attend(0, 0, 4)
    relay(1, DOWN)
    attend(1, 0, 2)
    relay_other(1, DOWN)
    attend(1, 2, 4)
    ready(1, OUT)
    ready(1, UP)
    ready(1, DOWN)
    feed_forward(1)

    @pl.loop(0, points // LANES)
    def _(i):
        at = block(i, LANES)
        keep[at] = chosen_cols(code_ref[at, 3:4].astype(jnp.int32), points)

    out_wait(1)
    seq_send_rows(2, cols[1])

    @pl.loop(0, points // LANES)
    def _(i):
        at = block(i, LANES)
        spread[at] = chosen_cols(code_ref[at, 2:3].astype(jnp.int32), slots)

    for i in range(QKV):
        to_partner(1, i).wait_send()
        to_sibling(1, i).wait_send()
    moved[...] = matmul(keep[...], cols[1]).astype(BF16)
    seq_receive(2)
    final_ref[...] = (moved[...].astype(F32) + matmul(spread[...], got[...])).astype(BF16)

    for l in range(2):
        for i in range(6):
            if l == 0 or i >= QKV:
                to_partner(l, i).wait_send()
                to_sibling(l, i).wait_send()
            forward(l, i).wait_send()
            if i >= QKV:
                to_neighbour(l, i).wait_send()
                forward_other(l, i).wait_send()
    for turn in range(3):
        for step in range(1, peers):
            seq_copy(turn, step).wait_send()


def on_device(peers, n_head, x_points, hilbert_index, w_qkv, w_out, w_up, w_down):
    points, cols = x_points.shape
    near = 3 * points // 16
    cap = points // (8 * peers)
    slots = 2 * near + peers * cap
    vmem = pl.BlockSpec(memory_space=pltpu.VMEM)
    w_qkv = jnp.transpose(w_qkv, (0, 2, 1, 3))

    width = cols * n_head
    own_rows = points // n_head
    hidden = w_up.shape[1] * n_head
    layers = w_up.shape[0]
    hbm = pl.BlockSpec(memory_space=pl.ANY)
    return pl.pallas_call(
        functools.partial(program_kernel, n_head, peers, near, cap),
        out_shape=jax.ShapeDtypeStruct((points, cols), BF16),
        in_specs=[hbm] * 5 + [vmem],
        out_specs=vmem,
        scratch_shapes=[
            pltpu.VMEM((layers, PATCH, width), BF16),
            pltpu.VMEM((layers, n_head // 2, 3, width, 2 * LANES), BF16),
            pltpu.VMEM((layers, width, width), BF16),
            pltpu.VMEM((layers, hidden, width), BF16),
            pltpu.VMEM((layers, hidden, width), BF16),
            pltpu.VMEM((PATCH, width), BF16),
            pltpu.VMEM((n_head, own_rows, LANES), BF16),
            pltpu.VMEM((n_head, PATCH, LANES), BF16),
            pltpu.VMEM((n_head, PATCH, 2 * LANES), BF16),
            pltpu.VMEM((own_rows, width), BF16),
            pltpu.VMEM((own_rows, width), BF16),
            pltpu.VMEM((own_rows, width), BF16),
            pltpu.VMEM((layers, points, cols), BF16),
            pltpu.VMEM((points, cols), BF16),
            pltpu.VMEM((slots, points), BF16),
            pltpu.VMEM((points, points), BF16),
            pltpu.VMEM((points, slots), BF16),
            pltpu.VMEM((3, 2 * near, cols), BF16),
            pltpu.VMEM((3, peers, cap, cols), BF16),
            pltpu.VMEM((3, 2 * near, cols), BF16),
            pltpu.VMEM((3, peers, cap, cols), BF16),
            pltpu.VMEM((slots, cols), BF16),
            pltpu.VMEM((slots, cols), F32),
            pltpu.VMEM((256, width), F32),
            pltpu.VMEM((points, LANES), F32),
            pltpu.SemaphoreType.DMA((layers, 6)),
            pltpu.SemaphoreType.DMA((layers, 6, 5)),
            pltpu.SemaphoreType.DMA((layers, 6, 5)),
            pltpu.SemaphoreType.DMA((layers, own_rows // 256, n_head)),
            pltpu.SemaphoreType.DMA((layers, own_rows // 256, n_head)),
            pltpu.SemaphoreType.DMA((3, peers)),
            pltpu.SemaphoreType.DMA((3, peers)),
        ],
        compiler_params=pltpu.CompilerParams(
            collective_id=0, has_side_effects=True, vmem_limit_bytes=60 * 1024 * 1024
        ),
        name="point_layers",
    )(x_points, w_qkv, w_out, w_up, w_down, hilbert_index.reshape(1, points))


def solution(mesh):
    return jax.shard_map(
        functools.partial(on_device, mesh.shape["seq"], mesh.shape["head"]),
        mesh=mesh,
        in_specs=(
            P("seq", "head"),
            P("seq"),
            P(None, None, None, "head"),
            P(None, "head", None),
            P(None, "head", None),
            P(None, "head", None),
        ),
        out_specs=P("seq", "head"),
        check_vma=False,
    )
```

```python
import functools
import math

import jax
import jax.numpy as jnp
from jax import lax
from jax.experimental import pallas as pl
from jax.experimental.pallas import tpu as pltpu
from jax.sharding import PartitionSpec as P

HEAD_DIM = 32
PATCH = 1024
EPS = 1e-05
LANES = 128
BASE = 64
MESH = pl.DeviceIdType.MESH
F32 = jnp.float32
BF16 = jnp.bfloat16


def block(index, size):
    return pl.ds(pl.multiple_of(index * size, size), size)


def norm(values):
    center = values - jnp.mean(values, axis=-1, keepdims=True)
    spread = jnp.mean(center * center, axis=-1, keepdims=True)
    return (center * lax.rsqrt(spread + EPS)).astype(BF16)


def matmul(a, b):
    return jnp.dot(a, b, preferred_element_type=F32)


def matmul_nt(a, b):
    return lax.dot_general(a, b, (((1,), (1,)), ((), ())), preferred_element_type=F32)


def gelu(x):
    return 0.5 * x * (1.0 + lax.erf(x * math.sqrt(0.5)))


def chosen_rows(count, base, index_row):
    slots = lax.broadcasted_iota(jnp.int32, (count, index_row.shape[1]), 0) + base
    return (slots == index_row).astype(F32).astype(BF16)


def chosen_cols(index_col, count):
    slots = lax.broadcasted_iota(jnp.int32, (index_col.shape[0], count), 1)
    return (slots == index_col).astype(F32).astype(BF16)


QKV, OUT, UP, DOWN = 2, 3, 4, 5


def program_kernel(
    n_head, peers, near, cap,
    x_ref, wqkv_ref, wout_ref, wup_ref, wdown_ref, index_ref,
    final_ref,
    rows, wqkv, wout, wup, wdown, normed, q, k, v, attended, mid_norm, result, cols, moved,
    pick, keep, spread, near_out, far_out, near_in, far_in, got, codes, partial, code_ref,
    local_sem, send_sem, recv_sem, out_send, out_recv, seq_send, seq_recv,
):
    me = lax.axis_index("head")
    seq = lax.axis_index("seq")
    side = lax.rem(seq, 2)
    neighbour = seq + 1 - 2 * side
    sibling = me + 1 - 2 * lax.rem(me, 2)
    partner = lax.rem(me + n_head // 2, n_head)
    half = lax.rem(me, 2)
    own_rows, width = result.shape
    points = moved.shape[0]
    slots = 2 * near + peers * cap
    chunk = PATCH // 2

    barrier = pltpu.get_barrier_semaphore()
    for step in range(1, n_head):
        to = lax.rem(me + step, n_head)
        pl.semaphore_signal(barrier, inc=1, device_id={"head": to}, device_id_type=MESH)
    for step in range(1, peers):
        to = lax.rem(seq + step, peers)
        pl.semaphore_signal(barrier, inc=1, device_id={"seq": to}, device_id_type=MESH)
    pl.semaphore_wait(barrier, n_head + peers - 2)

    def source(l, i, to):
        if i < 2:
            start = pl.multiple_of((to // 2) * PATCH + i * chunk, chunk)
            return (x_ref if l == 0 else moved).at[pl.ds(start, chunk)]
        return (wqkv_ref, wout_ref, wup_ref, wdown_ref)[i - QKV].at[l]

    def place(l, i, owner):
        if i < 2:
            return rows.at[l, pl.ds(i * chunk, chunk), block(owner, LANES)]
        if i == QKV:
            return wqkv.at[l, owner // 2, :, :, block(lax.rem(owner, 2), LANES)]
        ref = (wout, wup, wdown)[i - OUT]
        return ref.at[l, block(owner, ref.shape[1] // n_head)]

    def part(i, ref, which):
        if i < 2:
            return ref
        if i == QKV:
            return ref.at[:, block(which, ref.shape[1] // 2)]
        return ref.at[block(which, ref.shape[0] // 2)]

    def own(l, i):
        return pltpu.make_async_copy(source(l, i, me), place(l, i, me), local_sem.at[l, i])

    def remote(l, i, way, src, dst, device):
        return pltpu.make_async_remote_copy(
            src_ref=src,
            dst_ref=dst,
            send_sem=send_sem.at[l, i, way],
            recv_sem=recv_sem.at[l, i, way],
            device_id=device,
            device_id_type=MESH,
        )

    def to_partner(l, i):
        src = part(i, source(l, i, partner), side)
        return remote(l, i, 0, src, part(i, place(l, i, me), side), {"head": partner})

    def to_sibling(l, i):
        return remote(l, i, 1, source(l, i, sibling), place(l, i, me), {"head": sibling})

    def forward(l, i):
        ref = part(i, place(l, i, partner), side)
        return remote(l, i, 2, ref, ref, {"head": sibling})

    def to_neighbour(l, i):
        ref = part(i, place(l, i, partner), side)
        return remote(l, i, 3, ref, ref, {"seq": neighbour})

    def forward_other(l, i):
        ref = part(i, place(l, i, partner), 1 - side)
        return remote(l, i, 4, ref, ref, {"head": sibling})

    def send(l, i):
        to_partner(l, i).start()
        own(l, i).start()

    def relay(l, i):
        to_partner(l, i).wait_recv()
        if i >= QKV:
            to_neighbour(l, i).start()
        forward(l, i).start()

    def relay_other(l, i):
        to_neighbour(l, i).wait_recv()
        forward_other(l, i).start()

    def ready(l, i):
        own(l, i).wait()
        to_sibling(l, i).wait_recv()
        forward(l, i).wait_recv()
        if i >= QKV:
            forward_other(l, i).wait_recv()

    def seq_copy(turn, step):
        to = lax.rem(seq + step, peers)
        back = turn == 2
        if step == 1:
            at = pl.ds(near if back else 0, near)
            src, dst = near_out.at[turn, at], near_in.at[turn, at]
        elif step == peers - 1:
            at = pl.ds(0 if back else near, near)
            src, dst = near_out.at[turn, at], near_in.at[turn, at]
        else:
            src, dst = far_out.at[turn, to], far_in.at[turn, seq]
        return pltpu.make_async_remote_copy(
            src_ref=src,
            dst_ref=dst,
            send_sem=seq_send.at[turn, step],
            recv_sem=seq_recv.at[turn, step],
            device_id={"seq": to},
            device_id_type=MESH,
        )

    def seq_send_rows(turn, table):
        for lo in range(0, 2 * near, near):
            near_out[turn, lo : lo + near] = matmul(pick[lo : lo + near], table).astype(BF16)
            seq_copy(turn, (1 if lo == 0 else peers - 1) if turn != 2 else (peers - 1 if lo == 0 else 1)).start()
        packed = matmul(pick[2 * near :], table)
        for peer in range(peers):
            far_out[turn, peer] = packed[peer * cap : (peer + 1) * cap].astype(BF16)
        for step in range(2, peers - 1):
            seq_copy(turn, step).start()

    def seq_receive(turn):
        for step in range(1, peers):
            seq_copy(turn, step).wait_recv()
        for step in (0, 1, peers - 1):
            unused = lax.rem(seq + step, peers)
            far_in[turn, unused] = jnp.zeros(far_in.shape[2:], BF16)
        got[: 2 * near] = near_in[turn]
        for peer in range(peers):
            at = 2 * near + peer * cap
            got[at : at + cap] = far_in[turn, peer].astype(F32).astype(BF16)

    def normalise(l, i):
        @pl.loop(0, chunk // LANES)
        def _(j):
            at = pl.ds(pl.multiple_of(i * chunk + j * LANES, LANES), LANES)
            normed[at] = norm(rows[l, at].astype(F32))

    def keys_values(l, chip, i):
        at = pl.ds(i * chunk, chunk)
        keys = matmul(normed[at], wqkv[l, chip, 1]).astype(BF16)
        values = matmul(normed[at], wqkv[l, chip, 2]).astype(BF16)
        for part_of in range(2):
            cut = slice(part_of * LANES, (part_of + 1) * LANES)
            k[chip * 2 + part_of, at] = keys[:, cut]
            v[chip * 2 + part_of, at, :LANES] = values[:, cut]

    def queries(l, chip):
        scale = HEAD_DIM ** (-0.5) * math.log2(math.e)
        mine = pl.ds(pl.multiple_of(half * own_rows, own_rows), own_rows)
        found = (matmul(normed[mine], wqkv[l, chip, 0]) * scale).astype(BF16)
        for part_of in range(2):
            q[chip * 2 + part_of] = found[:, part_of * LANES : (part_of + 1) * LANES]

    def attend(first, count, between):
        owner = lax.broadcasted_iota(jnp.int32, (own_rows, LANES), 1) // HEAD_DIM

        @pl.loop(0, count)
        def _(step):
            for turn, action in between.items():
                pl.when(step == turn)(action)
            group = first + step
            query = q[group]

            def scores_of(head):
                return matmul_nt(jnp.where(owner == head, query, jnp.zeros_like(query)), k[group])

            total = jnp.zeros((own_rows, LANES), F32)
            norms = jnp.ones((own_rows, LANES), F32)
            scores = scores_of(0)
            for head in range(LANES // HEAD_DIM):
                following = scores_of(head + 1) if head + 1 < LANES // HEAD_DIM else None
                top = jnp.max(scores, axis=-1, keepdims=True)
                weights = jnp.exp2(scores - top).astype(BF16)
                mixed = matmul(weights, v[group])
                total = jnp.where(owner == head, mixed[:, :LANES], total)
                norms = jnp.where(owner == head, mixed[:, LANES:], norms)
                scores = following
            attended[:, block(group, LANES)] = (total / norms).astype(BF16)

    def out_copy(l, piece, step):
        to = lax.rem(me + step, n_head)
        at = pl.ds(pl.multiple_of(me * own_rows + piece * 256, 256), 256)
        return pltpu.make_async_remote_copy(
            src_ref=result.at[block(piece, 256), block(to, LANES)],
            dst_ref=cols.at[l, at],
            send_sem=out_send.at[l, piece, step],
            recv_sem=out_recv.at[l, piece, step],
            device_id={"head": to},
            device_id_type=MESH,
        )

    hidden = wup.shape[1]
    hidden_cols = 512

    def feed_forward(l):
        for piece in range(own_rows // 256):
            at = pl.ds(piece * 256, 256)
            mine = pl.ds(pl.multiple_of(half * own_rows + piece * 256, 256), 256)
            summed = (rows[l, mine].astype(F32) + matmul(attended[at], wout[l])).astype(BF16)
            total = summed.astype(F32)
            mid_norm[at] = norm(total)
            partial[...] = total

            @pl.loop(0, hidden // hidden_cols)
            def _(j):
                hid = block(j, hidden_cols)
                inner = gelu(matmul_nt(mid_norm[at], wup[l, hid])).astype(BF16)
                partial[...] += matmul(inner, wdown[l, hid])

            result[at] = partial[...].astype(BF16)
            for step in range(2, n_head):
                out_copy(l, piece, step).start()
            out_copy(l, piece, 1).start()
            cols[l, pl.ds(pl.multiple_of(me * own_rows + piece * 256, 256), 256)] = result[
                at, block(me, LANES)
            ]

    def out_wait(l):
        for piece in range(own_rows // 256):
            for step in range(1, n_head):
                out_copy(l, piece, step).wait()

    for i in range(6):
        send(0, i)
        if i < 3:
            to_sibling(0, i).start()
    send(1, QKV)
    send(1, OUT)

    where_to = index_ref[...]
    bounds = lax.broadcasted_iota(jnp.int32, (peers, points), 0) * points
    hot = jnp.where((where_to >= bounds) & (where_to < bounds + points), 1.0, 0.0)
    lower = lax.broadcasted_iota(jnp.int32, (LANES, LANES), 0)
    upper = lax.broadcasted_iota(jnp.int32, (LANES, LANES), 1)
    triangle = jnp.where(lower <= upper, 1.0, 0.0).astype(BF16)
    carried = jnp.zeros((peers, 1), F32)
    counts = []
    for at in range(0, points, LANES):
        piece = hot[:, at : at + LANES]
        counts.append(matmul(piece.astype(BF16), triangle) + carried)
        carried = carried + jnp.sum(piece, axis=1, keepdims=True)
    rank = jnp.sum(jnp.concatenate(counts, axis=1) * hot, axis=0, keepdims=True)
    rank = rank.astype(jnp.int32) - 1
    device_start = jnp.sum(hot * bounds.astype(F32), axis=0, keepdims=True).astype(jnp.int32)
    order = lax.broadcasted_iota(jnp.int32, (peers, points), 0).astype(F32)
    device = jnp.sum(hot * order, axis=0, keepdims=True).astype(jnp.int32)
    row = where_to - device_start
    following = lax.rem(seq + 1, peers)
    previous = lax.rem(seq + peers - 1, peers)
    slot = jnp.where(device == previous, near + rank, 2 * near + device * cap + rank)
    slot = jnp.where(device == following, rank, slot)
    slot = jnp.where(device == seq, -1, slot)
    kept = jnp.where(device == seq, row, -1)
    coded = row + BASE
    high = lax.shift_right_logical(coded, jnp.full_like(coded, BASE.bit_length() - 1))
    low = coded - high * BASE
    lane = lax.broadcasted_iota(jnp.int32, (LANES, points), 0)
    fields = jnp.where(lane == 2, slot, jnp.where(lane == 3, kept, 0))
    fields = jnp.where(lane == 0, high, jnp.where(lane == 1, low, fields))
    code_ref[...] = jnp.transpose(fields.astype(F32), (1, 0))

    @pl.loop(0, slots // LANES)
    def _(i):
        pick[block(i, LANES)] = chosen_rows(LANES, i * LANES, slot)

    relay(0, 0)
    seq_send_rows(0, code_ref[...].astype(BF16))
    relay(0, 1)
    for group in range(n_head):
        v[group, :, LANES:] = jnp.ones((PATCH, LANES), BF16)
    mine_chip = me // 2
    other_chip = partner // 2
    own(0, QKV).wait()
    to_sibling(0, QKV).wait_recv()
    ready(0, 0)
    normalise(0, 0)
    keys_values(0, mine_chip, 0)
    ready(0, 1)
    normalise(0, 1)
    keys_values(0, mine_chip, 1)
    queries(0, mine_chip)
    relay(0, QKV)
    to_sibling(0, OUT).start()
    seq_receive(0)
    codes[...] = got[...].astype(F32)
    turned = jnp.transpose(codes[...], (1, 0))
    target = (turned[0:1] * BASE + turned[1:2]).astype(jnp.int32) - BASE

    @pl.loop(0, points // LANES)
    def _(i):
        spread[block(i, LANES)] = chosen_rows(LANES, i * LANES, target)

    def relay_out():
        relay(0, OUT)
        to_sibling(0, UP).start()
        to_sibling(0, DOWN).start()

    attend(mine_chip * 2, 2, {1: relay_out})
    relay_other(0, QKV)
    relay_other(0, OUT)

    @pl.loop(0, points // LANES)
    def _(i):
        keep[block(i, LANES)] = chosen_rows(LANES, i * LANES, kept)

    relay(0, UP)
    forward(0, QKV).wait_recv()
    forward_other(0, QKV).wait_recv()
    for i in range(2):
        keys_values(0, other_chip, i)
    queries(0, other_chip)

    def relay_up_down():
        relay_other(0, UP)
        relay(0, DOWN)

    attend(other_chip * 2, 2, {1: relay_up_down})
    to_sibling(1, QKV).start()
    to_sibling(1, OUT).start()
    relay_other(0, DOWN)
    relay(1, QKV)
    ready(0, OUT)
    ready(0, UP)
    ready(0, DOWN)
    feed_forward(0)
    send(1, UP)
    to_sibling(1, UP).start()
    relay_other(1, QKV)
    relay(1, OUT)
    out_wait(0)

    seq_send_rows(1, cols[0])
    relay_other(1, OUT)
    moved[...] = matmul(keep[...], cols[0]).astype(BF16)
    seq_receive(1)
    moved[...] = (moved[...].astype(F32) + matmul(spread[...], got[...])).astype(BF16)

    for i in (0, 1, DOWN):
        send(1, i)
        to_sibling(1, i).start()

    @pl.loop(0, slots // LANES)
    def _(i):
        at = block(i, LANES)
        both = codes[at]
        place_col = (both[:, 0:1] * BASE + both[:, 1:2]).astype(jnp.int32) - BASE
        pick[at] = chosen_cols(place_col, points)

    relay(1, UP)
    relay(1, 0)
    relay(1, 1)
    ready(1, 0)
    normalise(1, 0)
    ready(1, QKV)
    for chip in range(n_head // 2):
        keys_values(1, chip, 0)
    ready(1, 1)
    normalise(1, 1)
    for chip in range(n_head // 2):
        keys_values(1, chip, 1)
    for chip in range(n_head // 2):
        queries(1, chip)
    attend(
        0,
        n_head,
        {
            1: lambda: relay_other(1, UP),
            2: lambda: relay(1, DOWN),
            n_head - 1: lambda: relay_other(1, DOWN),
        },
    )
    ready(1, OUT)
    ready(1, UP)
    ready(1, DOWN)
    feed_forward(1)

    @pl.loop(0, points // LANES)
    def _(i):
        at = block(i, LANES)
        keep[at] = chosen_cols(code_ref[at, 3:4].astype(jnp.int32), points)

    out_wait(1)
    seq_send_rows(2, cols[1])

    @pl.loop(0, points // LANES)
    def _(i):
        at = block(i, LANES)
        spread[at] = chosen_cols(code_ref[at, 2:3].astype(jnp.int32), slots)

    for i in range(QKV):
        to_partner(1, i).wait_send()
        to_sibling(1, i).wait_send()
    moved[...] = matmul(keep[...], cols[1]).astype(BF16)
    seq_receive(2)
    final_ref[...] = (moved[...].astype(F32) + matmul(spread[...], got[...])).astype(BF16)

    for l in range(2):
        for i in range(6):
            if l == 0 or i >= QKV:
                to_partner(l, i).wait_send()
                to_sibling(l, i).wait_send()
            forward(l, i).wait_send()
            if i >= QKV:
                to_neighbour(l, i).wait_send()
                forward_other(l, i).wait_send()
    for turn in range(3):
        for step in range(1, peers):
            seq_copy(turn, step).wait_send()


def on_device(peers, n_head, x_points, hilbert_index, w_qkv, w_out, w_up, w_down):
    points, cols = x_points.shape
    near = 3 * points // 16
    cap = points // (8 * peers)
    slots = 2 * near + peers * cap
    vmem = pl.BlockSpec(memory_space=pltpu.VMEM)
    w_qkv = jnp.transpose(w_qkv, (0, 2, 1, 3))

    width = cols * n_head
    own_rows = points // n_head
    hidden = w_up.shape[1] * n_head
    layers = w_up.shape[0]
    hbm = pl.BlockSpec(memory_space=pl.ANY)
    return pl.pallas_call(
        functools.partial(program_kernel, n_head, peers, near, cap),
        out_shape=jax.ShapeDtypeStruct((points, cols), BF16),
        in_specs=[hbm] * 5 + [vmem],
        out_specs=vmem,
        scratch_shapes=[
            pltpu.VMEM((layers, PATCH, width), BF16),
            pltpu.VMEM((layers, n_head // 2, 3, width, 2 * LANES), BF16),
            pltpu.VMEM((layers, width, width), BF16),
            pltpu.VMEM((layers, hidden, width), BF16),
            pltpu.VMEM((layers, hidden, width), BF16),
            pltpu.VMEM((PATCH, width), BF16),
            pltpu.VMEM((n_head, own_rows, LANES), BF16),
            pltpu.VMEM((n_head, PATCH, LANES), BF16),
            pltpu.VMEM((n_head, PATCH, 2 * LANES), BF16),
            pltpu.VMEM((own_rows, width), BF16),
            pltpu.VMEM((own_rows, width), BF16),
            pltpu.VMEM((own_rows, width), BF16),
            pltpu.VMEM((layers, points, cols), BF16),
            pltpu.VMEM((points, cols), BF16),
            pltpu.VMEM((slots, points), BF16),
            pltpu.VMEM((points, points), BF16),
            pltpu.VMEM((points, slots), BF16),
            pltpu.VMEM((3, 2 * near, cols), BF16),
            pltpu.VMEM((3, peers, cap, cols), BF16),
            pltpu.VMEM((3, 2 * near, cols), BF16),
            pltpu.VMEM((3, peers, cap, cols), BF16),
            pltpu.VMEM((slots, cols), BF16),
            pltpu.VMEM((slots, cols), F32),
            pltpu.VMEM((256, width), F32),
            pltpu.VMEM((points, LANES), F32),
            pltpu.SemaphoreType.DMA((layers, 6)),
            pltpu.SemaphoreType.DMA((layers, 6, 5)),
            pltpu.SemaphoreType.DMA((layers, 6, 5)),
            pltpu.SemaphoreType.DMA((layers, own_rows // 256, n_head)),
            pltpu.SemaphoreType.DMA((layers, own_rows // 256, n_head)),
            pltpu.SemaphoreType.DMA((3, peers)),
            pltpu.SemaphoreType.DMA((3, peers)),
        ],
        compiler_params=pltpu.CompilerParams(
            collective_id=0, has_side_effects=True, vmem_limit_bytes=60 * 1024 * 1024
        ),
        name="point_layers",
    )(x_points, w_qkv, w_out, w_up, w_down, hilbert_index.reshape(1, points))


def solution(mesh):
    return jax.shard_map(
        functools.partial(on_device, mesh.shape["seq"], mesh.shape["head"]),
        mesh=mesh,
        in_specs=(
            P("seq", "head"),
            P("seq"),
            P(None, None, None, "head"),
            P(None, "head", None),
            P(None, "head", None),
            P(None, "head", None),
        ),
        out_specs=P("seq", "head"),
        check_vma=False,
    )
```

```python
import functools
import math

import jax
import jax.numpy as jnp
from jax import lax
from jax.experimental import pallas as pl
from jax.experimental.pallas import tpu as pltpu
from jax.sharding import PartitionSpec as P

HEAD_DIM = 32
PATCH = 1024
EPS = 1e-05
LANES = 128
BASE = 64
MESH = pl.DeviceIdType.MESH
F32 = jnp.float32
BF16 = jnp.bfloat16


def block(index, size):
    return pl.ds(pl.multiple_of(index * size, size), size)


def norm(values):
    center = values - jnp.mean(values, axis=-1, keepdims=True)
    spread = jnp.mean(center * center, axis=-1, keepdims=True)
    return (center * lax.rsqrt(spread + EPS)).astype(BF16)


def matmul(a, b):
    return jnp.dot(a, b, preferred_element_type=F32)


def matmul_nt(a, b):
    return lax.dot_general(a, b, (((1,), (1,)), ((), ())), preferred_element_type=F32)


def gelu(x):
    return 0.5 * x * (1.0 + lax.erf(x * math.sqrt(0.5)))


def chosen_rows(count, base, index_row):
    slots = lax.broadcasted_iota(jnp.int32, (count, index_row.shape[1]), 0) + base
    return (slots == index_row).astype(F32).astype(BF16)


def chosen_cols(index_col, count):
    slots = lax.broadcasted_iota(jnp.int32, (index_col.shape[0], count), 1)
    return (slots == index_col).astype(F32).astype(BF16)


QKV, OUT = 2, 3
UP = (4, 6)
DOWN = (5, 7)
ITEMS = 8


def program_kernel(
    n_head, peers, near, cap,
    x_ref, wqkv_ref, wout_ref, wup_ref, wdown_ref, index_ref,
    final_ref,
    rows, wqkv, wout, wup, wdown, normed, q, k, v, attended, mid_norm, result, cols, moved,
    pick, keep, spread, near_out, far_out, near_in, far_in, got, codes, partial, code_ref,
    met, local_sem, send_sem, recv_sem, out_send, out_recv, seq_send, seq_recv,
):
    me = lax.axis_index("head")
    seq = lax.axis_index("seq")
    sibling = me + 1 - 2 * lax.rem(me, 2)
    partner = lax.rem(me + n_head // 2, n_head)
    half = lax.rem(me, 2)
    own_rows, width = result.shape
    points = moved.shape[0]
    slots = 2 * near + peers * cap
    chunk = PATCH // 2

    barrier = pltpu.get_barrier_semaphore()
    for step in range(1, n_head):
        to = lax.rem(me + step, n_head)
        pl.semaphore_signal(barrier, inc=1, device_id={"head": to}, device_id_type=MESH)
    rounds = peers.bit_length() - 1

    def across(turn):
        return seq + 2**turn - 2 ** (turn + 1) * lax.rem(seq // 2**turn, 2)

    def greet(sem, turn):
        pl.semaphore_signal(sem, inc=1, device_id={"seq": across(turn)}, device_id_type=MESH)

    for turn in range(rounds):
        greet(barrier, turn)
    pl.semaphore_wait(barrier, n_head - 1 + rounds)

    def entered(turn):
        pl.semaphore_wait(met.at[turn], 1)
        if turn + 1 < rounds:
            greet(met.at[turn + 1], turn + 1)

    def side_of(i):
        return lax.rem(seq // 2, 2) if i in (UP[1], DOWN[1]) else lax.rem(seq, 2)

    def neighbour_of(i):
        return across(1) if i in (UP[1], DOWN[1]) else across(0)

    hidden = wup.shape[1]
    hidden_half = hidden // n_head // 2

    def source(l, i, to):
        if i < 2:
            start = pl.multiple_of((to // 2) * PATCH + i * chunk, chunk)
            return (x_ref if l == 0 else moved).at[pl.ds(start, chunk)]
        if i in (QKV, OUT):
            return (wqkv_ref if i == QKV else wout_ref).at[l]
        ref, turn = (wup_ref, UP.index(i)) if i in UP else (wdown_ref, DOWN.index(i))
        return ref.at[l, pl.ds(turn * hidden_half, hidden_half)]

    def place(l, i, owner):
        if i < 2:
            return rows.at[l, pl.ds(i * chunk, chunk), block(owner, LANES)]
        if i == QKV:
            return wqkv.at[l, owner // 2, :, :, block(lax.rem(owner, 2), LANES)]
        if i == OUT:
            return wout.at[l, block(owner, wout.shape[1] // n_head)]
        ref, turn = (wup, UP.index(i)) if i in UP else (wdown, DOWN.index(i))
        return ref.at[l, block((owner // 2 * 2 + turn) * 2 + lax.rem(owner, 2), hidden_half)]

    def part(i, ref, which):
        if i < 2:
            return ref
        if i == QKV:
            return ref.at[:, block(which, ref.shape[1] // 2)]
        return ref.at[block(which, ref.shape[0] // 2)]

    def own(l, i):
        return pltpu.make_async_copy(source(l, i, me), place(l, i, me), local_sem.at[l, i])

    def remote(l, i, way, src, dst, device):
        return pltpu.make_async_remote_copy(
            src_ref=src,
            dst_ref=dst,
            send_sem=send_sem.at[l, i, way],
            recv_sem=recv_sem.at[l, i, way],
            device_id=device,
            device_id_type=MESH,
        )

    def to_partner(l, i):
        src = part(i, source(l, i, partner), side_of(i))
        return remote(l, i, 0, src, part(i, place(l, i, me), side_of(i)), {"head": partner})

    def to_sibling(l, i):
        return remote(l, i, 1, source(l, i, sibling), place(l, i, me), {"head": sibling})

    def forward(l, i):
        ref = part(i, place(l, i, partner), side_of(i))
        return remote(l, i, 2, ref, ref, {"head": sibling})

    def to_neighbour(l, i):
        ref = part(i, place(l, i, partner), side_of(i))
        return remote(l, i, 3, ref, ref, {"seq": neighbour_of(i)})

    def forward_other(l, i):
        ref = part(i, place(l, i, partner), 1 - side_of(i))
        return remote(l, i, 4, ref, ref, {"head": sibling})

    def send(l, i):
        to_partner(l, i).start()
        own(l, i).start()

    def relay(l, i):
        to_partner(l, i).wait_recv()
        if i >= QKV:
            to_neighbour(l, i).start()
        forward(l, i).start()

    def relay_other(l, i):
        to_neighbour(l, i).wait_recv()
        forward_other(l, i).start()

    def near_ready(l, i):
        own(l, i).wait()
        to_sibling(l, i).wait_recv()

    def far_ready(l, i):
        forward(l, i).wait_recv()
        if i >= QKV:
            forward_other(l, i).wait_recv()

    def ready(l, i):
        near_ready(l, i)
        far_ready(l, i)

    def seq_copy(turn, step):
        to = lax.rem(seq + step, peers)
        back = turn == 2
        if step == 1:
            at = pl.ds(near if back else 0, near)
            src, dst = near_out.at[turn, at], near_in.at[turn, at]
        elif step == peers - 1:
            at = pl.ds(0 if back else near, near)
            src, dst = near_out.at[turn, at], near_in.at[turn, at]
        else:
            src, dst = far_out.at[turn, to], far_in.at[turn, seq]
        return pltpu.make_async_remote_copy(
            src_ref=src,
            dst_ref=dst,
            send_sem=seq_send.at[turn, step],
            recv_sem=seq_recv.at[turn, step],
            device_id={"seq": to},
            device_id_type=MESH,
        )

    def seq_send_rows(turn, table):
        for lo in range(0, 2 * near, near):
            near_out[turn, lo : lo + near] = matmul(pick[lo : lo + near], table).astype(BF16)
            seq_copy(turn, (1 if lo == 0 else peers - 1) if turn != 2 else (peers - 1 if lo == 0 else 1)).start()
        packed = matmul(pick[2 * near :], table)
        for peer in range(peers):
            far_out[turn, peer] = packed[peer * cap : (peer + 1) * cap].astype(BF16)
        for step in range(2, peers - 1):
            seq_copy(turn, step).start()

    def seq_receive(turn):
        for step in range(1, peers):
            seq_copy(turn, step).wait_recv()
        for step in (0, 1, peers - 1):
            unused = lax.rem(seq + step, peers)
            far_in[turn, unused] = jnp.zeros(far_in.shape[2:], BF16)
        got[: 2 * near] = near_in[turn]
        for peer in range(peers):
            at = 2 * near + peer * cap
            got[at : at + cap] = far_in[turn, peer].astype(F32).astype(BF16)

    def normalise(l, i):
        @pl.loop(0, chunk // LANES)
        def _(j):
            at = pl.ds(pl.multiple_of(i * chunk + j * LANES, LANES), LANES)
            normed[at] = norm(rows[l, at].astype(F32))

    def keys_values(l, chip, i):
        at = pl.ds(i * chunk, chunk)
        keys = matmul(normed[at], wqkv[l, chip, 1]).astype(BF16)
        values = matmul(normed[at], wqkv[l, chip, 2]).astype(BF16)
        for part_of in range(2):
            cut = slice(part_of * LANES, (part_of + 1) * LANES)
            k[chip * 2 + part_of, at] = keys[:, cut]
            v[chip * 2 + part_of, at, :LANES] = values[:, cut]

    def queries(l, chip):
        scale = HEAD_DIM ** (-0.5) * math.log2(math.e)
        mine = pl.ds(pl.multiple_of(half * own_rows, own_rows), own_rows)
        found = (matmul(normed[mine], wqkv[l, chip, 0]) * scale).astype(BF16)
        for part_of in range(2):
            q[chip * 2 + part_of] = found[:, part_of * LANES : (part_of + 1) * LANES]

    def attend(first, count, between):
        owner = lax.broadcasted_iota(jnp.int32, (own_rows, LANES), 1) // HEAD_DIM

        @pl.loop(0, count)
        def _(step):
            for turn, action in between.items():
                pl.when(step == turn)(action)
            group = first + step
            query = q[group]

            def scores_of(head):
                return matmul_nt(jnp.where(owner == head, query, jnp.zeros_like(query)), k[group])

            total = jnp.zeros((own_rows, LANES), F32)
            norms = jnp.ones((own_rows, LANES), F32)
            scores = scores_of(0)
            for head in range(LANES // HEAD_DIM):
                following = scores_of(head + 1) if head + 1 < LANES // HEAD_DIM else None
                top = jnp.max(scores, axis=-1, keepdims=True)
                weights = jnp.exp2(scores - top).astype(BF16)
                mixed = matmul(weights, v[group])
                total = jnp.where(owner == head, mixed[:, :LANES], total)
                norms = jnp.where(owner == head, mixed[:, LANES:], norms)
                scores = following
            attended[:, block(group, LANES)] = (total / norms).astype(BF16)

    def out_copy(l, piece, step):
        to = lax.rem(me + step, n_head)
        at = pl.ds(pl.multiple_of(me * own_rows + piece * 256, 256), 256)
        return pltpu.make_async_remote_copy(
            src_ref=result.at[block(piece, 256), block(to, LANES)],
            dst_ref=cols.at[l, at],
            send_sem=out_send.at[l, piece, step],
            recv_sem=out_recv.at[l, piece, step],
            device_id={"head": to},
            device_id_type=MESH,
        )

    hidden_cols = hidden // n_head

    def feed_forward(l, between):
        for piece in range(own_rows // 256):
            at = pl.ds(piece * 256, 256)
            mine = pl.ds(pl.multiple_of(half * own_rows + piece * 256, 256), 256)
            summed = (rows[l, mine].astype(F32) + matmul(attended[at], wout[l])).astype(BF16)
            total = summed.astype(F32)
            mid_norm[at] = norm(total)
            partial[...] = total

            @pl.loop(0, n_head)
            def _(j):
                for turn, action in between[piece].items():
                    pl.when(j == turn)(action)
                hid = block(lax.rem(me // 2 * 2 + j, n_head), hidden_cols)
                inner = gelu(matmul_nt(mid_norm[at], wup[l, hid])).astype(BF16)
                partial[...] += matmul(inner, wdown[l, hid])

            result[at] = partial[...].astype(BF16)
            for step in range(2, n_head):
                out_copy(l, piece, step).start()
            out_copy(l, piece, 1).start()
            cols[l, pl.ds(pl.multiple_of(me * own_rows + piece * 256, 256), 256)] = result[
                at, block(me, LANES)
            ]

    def out_wait(l):
        for piece in range(own_rows // 256):
            for step in range(1, n_head):
                out_copy(l, piece, step).wait()

    greet(met.at[0], 0)
    for i in range(ITEMS):
        send(0, i)
        if i <= QKV:
            to_sibling(0, i).start()
    send(1, QKV)
    send(1, OUT)

    where_to = index_ref[...]
    bounds = lax.broadcasted_iota(jnp.int32, (peers, points), 0) * points
    hot = jnp.where((where_to >= bounds) & (where_to < bounds + points), 1.0, 0.0)
    lower = lax.broadcasted_iota(jnp.int32, (LANES, LANES), 0)
    upper = lax.broadcasted_iota(jnp.int32, (LANES, LANES), 1)
    triangle = jnp.where(lower <= upper, 1.0, 0.0).astype(BF16)
    carried = jnp.zeros((peers, 1), F32)
    counts = []
    for at in range(0, points, LANES):
        piece = hot[:, at : at + LANES]
        counts.append(matmul(piece.astype(BF16), triangle) + carried)
        carried = carried + jnp.sum(piece, axis=1, keepdims=True)
    rank = jnp.sum(jnp.concatenate(counts, axis=1) * hot, axis=0, keepdims=True)
    rank = rank.astype(jnp.int32) - 1
    device_start = jnp.sum(hot * bounds.astype(F32), axis=0, keepdims=True).astype(jnp.int32)
    order = lax.broadcasted_iota(jnp.int32, (peers, points), 0).astype(F32)
    device = jnp.sum(hot * order, axis=0, keepdims=True).astype(jnp.int32)
    row = where_to - device_start
    following = lax.rem(seq + 1, peers)
    previous = lax.rem(seq + peers - 1, peers)
    slot = jnp.where(device == previous, near + rank, 2 * near + device * cap + rank)
    slot = jnp.where(device == following, rank, slot)
    slot = jnp.where(device == seq, -1, slot)
    kept = jnp.where(device == seq, row, -1)
    coded = row + BASE
    high = lax.shift_right_logical(coded, jnp.full_like(coded, BASE.bit_length() - 1))
    low = coded - high * BASE
    lane = lax.broadcasted_iota(jnp.int32, (LANES, points), 0)
    fields = jnp.where(lane == 2, slot, jnp.where(lane == 3, kept, 0))
    fields = jnp.where(lane == 0, high, jnp.where(lane == 1, low, fields))
    code_ref[...] = jnp.transpose(fields.astype(F32), (1, 0))

    @pl.loop(0, slots // LANES)
    def _(i):
        pick[block(i, LANES)] = chosen_rows(LANES, i * LANES, slot)

    relay(0, 0)
    for turn in range(rounds):
        entered(turn)
    seq_send_rows(0, code_ref[...].astype(BF16))
    relay(0, 1)
    for group in range(n_head):
        v[group, :, LANES:] = jnp.ones((PATCH, LANES), BF16)
    mine_chip = me // 2
    other_chip = partner // 2
    near_ready(0, QKV)
    ready(0, 0)
    normalise(0, 0)
    keys_values(0, mine_chip, 0)
    ready(0, 1)
    normalise(0, 1)
    keys_values(0, mine_chip, 1)
    queries(0, mine_chip)
    relay(0, QKV)
    for i in range(OUT, ITEMS):
        to_sibling(0, i).start()
    seq_receive(0)
    codes[...] = got[...].astype(F32)
    turned = jnp.transpose(codes[...], (1, 0))
    target = (turned[0:1] * BASE + turned[1:2]).astype(jnp.int32) - BASE

    @pl.loop(0, points // LANES)
    def _(i):
        spread[block(i, LANES)] = chosen_rows(LANES, i * LANES, target)

    attend(mine_chip * 2, 2, {1: lambda: relay(0, OUT)})
    relay_other(0, QKV)
    relay(0, UP[0])
    relay_other(0, OUT)

    @pl.loop(0, points // LANES)
    def _(i):
        keep[block(i, LANES)] = chosen_rows(LANES, i * LANES, kept)

    relay(0, DOWN[0])
    far_ready(0, QKV)
    for i in range(2):
        keys_values(0, other_chip, i)
    queries(0, other_chip)
    relay(0, UP[1])

    def relay_last():
        relay(0, DOWN[1])
        relay_other(0, UP[0])

    attend(other_chip * 2, 2, {1: relay_last})
    relay_other(0, DOWN[0])
    to_sibling(1, QKV).start()
    to_sibling(1, OUT).start()
    ready(0, OUT)
    for i in UP + DOWN:
        near_ready(0, i)

    def first_far():
        far_ready(0, UP[0])
        far_ready(0, DOWN[0])
        relay_other(0, UP[1])

    def last_far():
        relay_other(0, DOWN[1])
        far_ready(0, UP[1])
        far_ready(0, DOWN[1])

    feed_forward(
        0,
        (
            {n_head // 2: first_far, n_head - 1: last_far},
            {0: lambda: relay(1, QKV), 2: lambda: relay(1, OUT)},
        ),
    )
    for i in range(OUT + 1, ITEMS):
        send(1, i)
        to_sibling(1, i).start()
    out_wait(0)

    seq_send_rows(1, cols[0])
    relay_other(1, QKV)
    relay_other(1, OUT)
    moved[...] = matmul(keep[...], cols[0]).astype(BF16)
    seq_receive(1)
    moved[...] = (moved[...].astype(F32) + matmul(spread[...], got[...])).astype(BF16)

    for i in range(2):
        send(1, i)
        to_sibling(1, i).start()
    relay(1, UP[0])
    relay(1, UP[1])

    @pl.loop(0, slots // LANES)
    def _(i):
        at = block(i, LANES)
        both = codes[at]
        place_col = (both[:, 0:1] * BASE + both[:, 1:2]).astype(jnp.int32) - BASE
        pick[at] = chosen_cols(place_col, points)

    relay(1, DOWN[0])
    relay(1, DOWN[1])
    relay(1, 0)
    relay(1, 1)
    ready(1, 0)
    normalise(1, 0)
    ready(1, QKV)
    for chip in range(n_head // 2):
        keys_values(1, chip, 0)
    ready(1, 1)
    normalise(1, 1)
    for chip in range(n_head // 2):
        keys_values(1, chip, 1)
    for chip in range(n_head // 2):
        queries(1, chip)
    def relay_ups():
        for i in UP:
            relay_other(1, i)

    def relay_downs():
        for i in DOWN:
            relay_other(1, i)

    attend(0, n_head, {1: relay_ups, 2: relay_downs})
    for i in range(OUT, ITEMS):
        ready(1, i)
    feed_forward(1, ({}, {}))

    @pl.loop(0, points // LANES)
    def _(i):
        at = block(i, LANES)
        keep[at] = chosen_cols(code_ref[at, 3:4].astype(jnp.int32), points)

    out_wait(1)
    seq_send_rows(2, cols[1])

    @pl.loop(0, points // LANES)
    def _(i):
        at = block(i, LANES)
        spread[at] = chosen_cols(code_ref[at, 2:3].astype(jnp.int32), slots)

    for i in range(QKV):
        to_partner(1, i).wait_send()
        to_sibling(1, i).wait_send()
    moved[...] = matmul(keep[...], cols[1]).astype(BF16)
    seq_receive(2)
    final_ref[...] = (moved[...].astype(F32) + matmul(spread[...], got[...])).astype(BF16)

    for l in range(2):
        for i in range(ITEMS):
            if l == 0 or i >= QKV:
                to_partner(l, i).wait_send()
                to_sibling(l, i).wait_send()
            forward(l, i).wait_send()
            if i >= QKV:
                to_neighbour(l, i).wait_send()
                forward_other(l, i).wait_send()
    for turn in range(3):
        for step in range(1, peers):
            seq_copy(turn, step).wait_send()


def on_device(peers, n_head, x_points, hilbert_index, w_qkv, w_out, w_up, w_down):
    points, cols = x_points.shape
    near = 3 * points // 16
    cap = points // (8 * peers)
    slots = 2 * near + peers * cap
    vmem = pl.BlockSpec(memory_space=pltpu.VMEM)
    w_qkv = jnp.transpose(w_qkv, (0, 2, 1, 3))

    width = cols * n_head
    own_rows = points // n_head
    hidden = w_up.shape[1] * n_head
    layers = w_up.shape[0]
    hbm = pl.BlockSpec(memory_space=pl.ANY)
    return pl.pallas_call(
        functools.partial(program_kernel, n_head, peers, near, cap),
        out_shape=jax.ShapeDtypeStruct((points, cols), BF16),
        in_specs=[hbm] * 5 + [vmem],
        out_specs=vmem,
        scratch_shapes=[
            pltpu.VMEM((layers, PATCH, width), BF16),
            pltpu.VMEM((layers, n_head // 2, 3, width, 2 * LANES), BF16),
            pltpu.VMEM((layers, width, width), BF16),
            pltpu.VMEM((layers, hidden, width), BF16),
            pltpu.VMEM((layers, hidden, width), BF16),
            pltpu.VMEM((PATCH, width), BF16),
            pltpu.VMEM((n_head, own_rows, LANES), BF16),
            pltpu.VMEM((n_head, PATCH, LANES), BF16),
            pltpu.VMEM((n_head, PATCH, 2 * LANES), BF16),
            pltpu.VMEM((own_rows, width), BF16),
            pltpu.VMEM((own_rows, width), BF16),
            pltpu.VMEM((own_rows, width), BF16),
            pltpu.VMEM((layers, points, cols), BF16),
            pltpu.VMEM((points, cols), BF16),
            pltpu.VMEM((slots, points), BF16),
            pltpu.VMEM((points, points), BF16),
            pltpu.VMEM((points, slots), BF16),
            pltpu.VMEM((3, 2 * near, cols), BF16),
            pltpu.VMEM((3, peers, cap, cols), BF16),
            pltpu.VMEM((3, 2 * near, cols), BF16),
            pltpu.VMEM((3, peers, cap, cols), BF16),
            pltpu.VMEM((slots, cols), BF16),
            pltpu.VMEM((slots, cols), F32),
            pltpu.VMEM((256, width), F32),
            pltpu.VMEM((points, LANES), F32),
            pltpu.SemaphoreType.REGULAR((peers.bit_length() - 1,)),
            pltpu.SemaphoreType.DMA((layers, ITEMS)),
            pltpu.SemaphoreType.DMA((layers, ITEMS, 5)),
            pltpu.SemaphoreType.DMA((layers, ITEMS, 5)),
            pltpu.SemaphoreType.DMA((layers, own_rows // 256, n_head)),
            pltpu.SemaphoreType.DMA((layers, own_rows // 256, n_head)),
            pltpu.SemaphoreType.DMA((3, peers)),
            pltpu.SemaphoreType.DMA((3, peers)),
        ],
        compiler_params=pltpu.CompilerParams(
            collective_id=0, has_side_effects=True, vmem_limit_bytes=60 * 1024 * 1024
        ),
        name="point_layers",
    )(x_points, w_qkv, w_out, w_up, w_down, hilbert_index.reshape(1, points))


def solution(mesh):
    return jax.shard_map(
        functools.partial(on_device, mesh.shape["seq"], mesh.shape["head"]),
        mesh=mesh,
        in_specs=(
            P("seq", "head"),
            P("seq"),
            P(None, None, None, "head"),
            P(None, "head", None),
            P(None, "head", None),
            P(None, "head", None),
        ),
        out_specs=P("seq", "head"),
        check_vma=False,
    )
```

```python
import functools
import math

import jax
import jax.numpy as jnp
from jax import lax
from jax.experimental import pallas as pl
from jax.experimental.pallas import tpu as pltpu
from jax.sharding import PartitionSpec as P

HEAD_DIM = 32
PATCH = 1024
EPS = 1e-05
LANES = 128
BASE = 64
MESH = pl.DeviceIdType.MESH
F32 = jnp.float32
BF16 = jnp.bfloat16


def block(index, size):
    return pl.ds(pl.multiple_of(index * size, size), size)


def norm(values):
    center = values - jnp.mean(values, axis=-1, keepdims=True)
    spread = jnp.mean(center * center, axis=-1, keepdims=True)
    return (center * lax.rsqrt(spread + EPS)).astype(BF16)


def matmul(a, b):
    return jnp.dot(a, b, preferred_element_type=F32)


def matmul_nt(a, b):
    return lax.dot_general(a, b, (((1,), (1,)), ((), ())), preferred_element_type=F32)


def gelu(x):
    return 0.5 * x * (1.0 + lax.erf(x * math.sqrt(0.5)))


def chosen_rows(count, base, index_row):
    slots = lax.broadcasted_iota(jnp.int32, (count, index_row.shape[1]), 0) + base
    return (slots == index_row).astype(F32).astype(BF16)


def chosen_cols(index_col, count):
    slots = lax.broadcasted_iota(jnp.int32, (index_col.shape[0], count), 1)
    return (slots == index_col).astype(F32).astype(BF16)


QKV, OUT = 2, 3
UP = (4, 6)
DOWN = (5, 7)
ITEMS = 8


def program_kernel(
    n_head, peers, near, cap,
    x_ref, wqkv_ref, wout_ref, wup_ref, wdown_ref, index_ref,
    final_ref,
    rows, wqkv, wout, wup, wdown, normed, q, k, v, attended, mid_norm, result, cols, moved,
    pick, keep, spread, near_out, far_out, near_in, far_in, got, codes, partial, code_ref,
    met, local_sem, send_sem, recv_sem, out_send, out_recv, seq_send, seq_recv,
):
    me = lax.axis_index("head")
    seq = lax.axis_index("seq")
    sibling = me + 1 - 2 * lax.rem(me, 2)
    partner = lax.rem(me + n_head // 2, n_head)
    half = lax.rem(me, 2)
    own_rows, width = result.shape
    points = moved.shape[0]
    slots = 2 * near + peers * cap
    chunk = PATCH // 2

    barrier = pltpu.get_barrier_semaphore()
    for step in range(1, n_head):
        to = lax.rem(me + step, n_head)
        pl.semaphore_signal(barrier, inc=1, device_id={"head": to}, device_id_type=MESH)
    rounds = peers.bit_length() - 1

    def across(turn):
        return seq + 2**turn - 2 ** (turn + 1) * lax.rem(seq // 2**turn, 2)

    def greet(sem, turn):
        pl.semaphore_signal(sem, inc=1, device_id={"seq": across(turn)}, device_id_type=MESH)

    for turn in range(rounds):
        greet(barrier, turn)
    pl.semaphore_wait(barrier, n_head - 1 + rounds)

    def entered(turn):
        pl.semaphore_wait(met.at[turn], 1)
        if turn + 1 < rounds:
            greet(met.at[turn + 1], turn + 1)

    def side_of(i):
        return lax.rem(seq // 2, 2) if i in (UP[1], DOWN[1]) else lax.rem(seq, 2)

    def neighbour_of(i):
        return across(1) if i in (UP[1], DOWN[1]) else across(0)

    hidden = wup.shape[1]
    hidden_half = hidden // n_head // 2

    def source(l, i, to):
        if i < 2:
            start = pl.multiple_of((to // 2) * PATCH + i * chunk, chunk)
            return (x_ref if l == 0 else moved).at[pl.ds(start, chunk)]
        if i in (QKV, OUT):
            return (wqkv_ref if i == QKV else wout_ref).at[l]
        ref, turn = (wup_ref, UP.index(i)) if i in UP else (wdown_ref, DOWN.index(i))
        return ref.at[l, pl.ds(turn * hidden_half, hidden_half)]

    def place(l, i, owner):
        if i < 2:
            return rows.at[l, pl.ds(i * chunk, chunk), block(owner, LANES)]
        if i == QKV:
            return wqkv.at[l, owner // 2, :, :, block(lax.rem(owner, 2), LANES)]
        if i == OUT:
            return wout.at[l, block(owner, wout.shape[1] // n_head)]
        ref, turn = (wup, UP.index(i)) if i in UP else (wdown, DOWN.index(i))
        return ref.at[l, block((owner // 2 * 2 + turn) * 2 + lax.rem(owner, 2), hidden_half)]

    def part(i, ref, which):
        if i < 2:
            return ref
        if i == QKV:
            return ref.at[:, block(which, ref.shape[1] // 2)]
        return ref.at[block(which, ref.shape[0] // 2)]

    def own(l, i):
        return pltpu.make_async_copy(source(l, i, me), place(l, i, me), local_sem.at[l, i])

    def remote(l, i, way, src, dst, device):
        return pltpu.make_async_remote_copy(
            src_ref=src,
            dst_ref=dst,
            send_sem=send_sem.at[l, i, way],
            recv_sem=recv_sem.at[l, i, way],
            device_id=device,
            device_id_type=MESH,
        )

    def to_partner(l, i):
        src = part(i, source(l, i, partner), side_of(i))
        return remote(l, i, 0, src, part(i, place(l, i, me), side_of(i)), {"head": partner})

    def to_sibling(l, i):
        return remote(l, i, 1, source(l, i, sibling), place(l, i, me), {"head": sibling})

    def forward(l, i):
        ref = part(i, place(l, i, partner), side_of(i))
        return remote(l, i, 2, ref, ref, {"head": sibling})

    def to_neighbour(l, i):
        ref = part(i, place(l, i, partner), side_of(i))
        return remote(l, i, 3, ref, ref, {"seq": neighbour_of(i)})

    def forward_other(l, i):
        ref = part(i, place(l, i, partner), 1 - side_of(i))
        return remote(l, i, 4, ref, ref, {"head": sibling})

    def send(l, i):
        to_partner(l, i).start()
        own(l, i).start()

    def relay(l, i):
        to_partner(l, i).wait_recv()
        if i >= QKV:
            to_neighbour(l, i).start()
        forward(l, i).start()

    def relay_other(l, i):
        to_neighbour(l, i).wait_recv()
        forward_other(l, i).start()

    def near_ready(l, i):
        own(l, i).wait()
        to_sibling(l, i).wait_recv()

    def far_ready(l, i):
        forward(l, i).wait_recv()
        if i >= QKV:
            forward_other(l, i).wait_recv()

    def ready(l, i):
        near_ready(l, i)
        far_ready(l, i)

    def seq_copy(turn, step):
        to = lax.rem(seq + step, peers)
        back = turn == 2
        if step == 1:
            at = pl.ds(near if back else 0, near)
            src, dst = near_out.at[turn, at], near_in.at[turn, at]
        elif step == peers - 1:
            at = pl.ds(0 if back else near, near)
            src, dst = near_out.at[turn, at], near_in.at[turn, at]
        else:
            src, dst = far_out.at[turn, to], far_in.at[turn, seq]
        return pltpu.make_async_remote_copy(
            src_ref=src,
            dst_ref=dst,
            send_sem=seq_send.at[turn, step],
            recv_sem=seq_recv.at[turn, step],
            device_id={"seq": to},
            device_id_type=MESH,
        )

    def seq_send_rows(turn, table):
        for lo in range(0, 2 * near, near):
            near_out[turn, lo : lo + near] = matmul(pick[lo : lo + near], table).astype(BF16)
            seq_copy(turn, (1 if lo == 0 else peers - 1) if turn != 2 else (peers - 1 if lo == 0 else 1)).start()
        packed = matmul(pick[2 * near :], table)
        for peer in range(peers):
            far_out[turn, peer] = packed[peer * cap : (peer + 1) * cap].astype(BF16)
        for step in range(2, peers - 1):
            seq_copy(turn, step).start()

    def seq_receive(turn):
        for step in range(1, peers):
            seq_copy(turn, step).wait_recv()
        for step in (0, 1, peers - 1):
            unused = lax.rem(seq + step, peers)
            far_in[turn, unused] = jnp.zeros(far_in.shape[2:], BF16)
        got[: 2 * near] = near_in[turn]
        for peer in range(peers):
            at = 2 * near + peer * cap
            got[at : at + cap] = far_in[turn, peer].astype(F32).astype(BF16)

    def normalise(l, i):
        @pl.loop(0, chunk // LANES)
        def _(j):
            at = pl.ds(pl.multiple_of(i * chunk + j * LANES, LANES), LANES)
            normed[at] = norm(rows[l, at].astype(F32))

    def keys_values(l, chip, i):
        at = pl.ds(i * chunk, chunk)
        keys = matmul(normed[at], wqkv[l, chip, 1]).astype(BF16)
        values = matmul(normed[at], wqkv[l, chip, 2]).astype(BF16)
        for part_of in range(2):
            cut = slice(part_of * LANES, (part_of + 1) * LANES)
            k[chip * 2 + part_of, at] = keys[:, cut]
            v[chip * 2 + part_of, at, :LANES] = values[:, cut]

    def queries(l, chip):
        scale = HEAD_DIM ** (-0.5) * math.log2(math.e)
        mine = pl.ds(pl.multiple_of(half * own_rows, own_rows), own_rows)
        found = (matmul(normed[mine], wqkv[l, chip, 0]) * scale).astype(BF16)
        for part_of in range(2):
            q[chip * 2 + part_of] = found[:, part_of * LANES : (part_of + 1) * LANES]

    def attend(first, count, between):
        owner = lax.broadcasted_iota(jnp.int32, (own_rows, LANES), 1) // HEAD_DIM

        @pl.loop(0, count)
        def _(step):
            for turn, action in between.items():
                pl.when(step == turn)(action)
            group = first + step
            query = q[group]

            def scores_of(head):
                return matmul_nt(jnp.where(owner == head, query, jnp.zeros_like(query)), k[group])

            total = jnp.zeros((own_rows, LANES), F32)
            norms = jnp.ones((own_rows, LANES), F32)
            scores = scores_of(0)
            for head in range(LANES // HEAD_DIM):
                following = scores_of(head + 1) if head + 1 < LANES // HEAD_DIM else None
                top = jnp.max(scores, axis=-1, keepdims=True)
                weights = jnp.exp2(scores - top).astype(BF16)
                mixed = matmul(weights, v[group])
                total = jnp.where(owner == head, mixed[:, :LANES], total)
                norms = jnp.where(owner == head, mixed[:, LANES:], norms)
                scores = following
            attended[:, block(group, LANES)] = (total / norms).astype(BF16)

    def out_copy(l, piece, step):
        to = lax.rem(me + step, n_head)
        at = pl.ds(pl.multiple_of(me * own_rows + piece * 256, 256), 256)
        return pltpu.make_async_remote_copy(
            src_ref=result.at[block(piece, 256), block(to, LANES)],
            dst_ref=cols.at[l, at],
            send_sem=out_send.at[l, piece, step],
            recv_sem=out_recv.at[l, piece, step],
            device_id={"head": to},
            device_id_type=MESH,
        )

    hidden_cols = hidden // n_head

    def feed_forward(l, between):
        for piece in range(own_rows // 256):
            at = pl.ds(piece * 256, 256)
            mine = pl.ds(pl.multiple_of(half * own_rows + piece * 256, 256), 256)
            summed = (rows[l, mine].astype(F32) + matmul(attended[at], wout[l])).astype(BF16)
            total = summed.astype(F32)
            mid_norm[at] = norm(total)
            partial[...] = total

            @pl.loop(0, n_head // 2)
            def _(j):
                for turn, action in between[piece].items():
                    pl.when(j == turn // 2)(action)
                first = block(lax.rem(me // 2 * 2 + 2 * j, n_head), hidden_cols)
                second = block(lax.rem(me // 2 * 2 + 2 * j + 1, n_head), hidden_cols)
                raised = matmul_nt(mid_norm[at], wup[l, first])
                later = matmul_nt(mid_norm[at], wup[l, second])
                lowered = matmul(gelu(raised).astype(BF16), wdown[l, first])
                partial[...] += lowered + matmul(gelu(later).astype(BF16), wdown[l, second])

            result[at] = partial[...].astype(BF16)
            for step in range(2, n_head):
                out_copy(l, piece, step).start()
            out_copy(l, piece, 1).start()
            cols[l, pl.ds(pl.multiple_of(me * own_rows + piece * 256, 256), 256)] = result[
                at, block(me, LANES)
            ]

    def out_wait(l):
        for piece in range(own_rows // 256):
            for step in range(1, n_head):
                out_copy(l, piece, step).wait()

    greet(met.at[0], 0)
    for i in range(ITEMS):
        send(0, i)
        if i <= QKV:
            to_sibling(0, i).start()
    send(1, QKV)
    send(1, OUT)

    where_to = index_ref[...]
    bounds = lax.broadcasted_iota(jnp.int32, (peers, points), 0) * points
    hot = jnp.where((where_to >= bounds) & (where_to < bounds + points), 1.0, 0.0)
    lower = lax.broadcasted_iota(jnp.int32, (LANES, LANES), 0)
    upper = lax.broadcasted_iota(jnp.int32, (LANES, LANES), 1)
    triangle = jnp.where(lower <= upper, 1.0, 0.0).astype(BF16)
    carried = jnp.zeros((peers, 1), F32)
    counts = []
    for at in range(0, points, LANES):
        piece = hot[:, at : at + LANES]
        counts.append(matmul(piece.astype(BF16), triangle) + carried)
        carried = carried + jnp.sum(piece, axis=1, keepdims=True)
    rank = jnp.sum(jnp.concatenate(counts, axis=1) * hot, axis=0, keepdims=True)
    rank = rank.astype(jnp.int32) - 1
    device_start = jnp.sum(hot * bounds.astype(F32), axis=0, keepdims=True).astype(jnp.int32)
    order = lax.broadcasted_iota(jnp.int32, (peers, points), 0).astype(F32)
    device = jnp.sum(hot * order, axis=0, keepdims=True).astype(jnp.int32)
    row = where_to - device_start
    following = lax.rem(seq + 1, peers)
    previous = lax.rem(seq + peers - 1, peers)
    slot = jnp.where(device == previous, near + rank, 2 * near + device * cap + rank)
    slot = jnp.where(device == following, rank, slot)
    slot = jnp.where(device == seq, -1, slot)
    kept = jnp.where(device == seq, row, -1)
    coded = row + BASE
    high = lax.shift_right_logical(coded, jnp.full_like(coded, BASE.bit_length() - 1))
    low = coded - high * BASE
    lane = lax.broadcasted_iota(jnp.int32, (LANES, points), 0)
    fields = jnp.where(lane == 2, slot, jnp.where(lane == 3, kept, 0))
    fields = jnp.where(lane == 0, high, jnp.where(lane == 1, low, fields))
    code_ref[...] = jnp.transpose(fields.astype(F32), (1, 0))

    @pl.loop(0, slots // LANES)
    def _(i):
        pick[block(i, LANES)] = chosen_rows(LANES, i * LANES, slot)

    for turn in range(rounds):
        entered(turn)
    seq_send_rows(0, code_ref[...].astype(BF16))

    @pl.loop(0, points // LANES)
    def _(i):
        keep[block(i, LANES)] = chosen_rows(LANES, i * LANES, kept)

    relay(0, 0)
    for group in range(n_head):
        v[group, :, LANES:] = jnp.ones((PATCH, LANES), BF16)
    mine_chip = me // 2
    other_chip = partner // 2
    near_ready(0, QKV)
    ready(0, 0)
    normalise(0, 0)
    keys_values(0, mine_chip, 0)
    relay(0, 1)
    ready(0, 1)
    normalise(0, 1)
    keys_values(0, mine_chip, 1)
    queries(0, mine_chip)
    seq_receive(0)
    codes[...] = got[...].astype(F32)
    turned = jnp.transpose(codes[...], (1, 0))
    target = (turned[0:1] * BASE + turned[1:2]).astype(jnp.int32) - BASE

    @pl.loop(0, points // LANES)
    def _(i):
        spread[block(i, LANES)] = chosen_rows(LANES, i * LANES, target)

    relay(0, QKV)
    for i in range(OUT, ITEMS):
        to_sibling(0, i).start()
    attend(mine_chip * 2, 2, {1: lambda: relay(0, OUT)})
    relay_other(0, QKV)
    relay(0, UP[0])
    relay_other(0, OUT)

    relay(0, DOWN[0])
    far_ready(0, QKV)
    for i in range(2):
        keys_values(0, other_chip, i)
    queries(0, other_chip)
    relay(0, UP[1])

    def relay_last():
        relay(0, DOWN[1])
        relay_other(0, UP[0])

    attend(other_chip * 2, 2, {1: relay_last})
    relay_other(0, DOWN[0])
    to_sibling(1, QKV).start()
    to_sibling(1, OUT).start()
    ready(0, OUT)
    for i in UP + DOWN:
        near_ready(0, i)

    def first_far():
        far_ready(0, UP[0])
        far_ready(0, DOWN[0])
        relay_other(0, UP[1])

    def last_far():
        relay_other(0, DOWN[1])
        far_ready(0, UP[1])
        far_ready(0, DOWN[1])

    feed_forward(
        0,
        (
            {n_head // 2: first_far, n_head - 1: last_far},
            {0: lambda: relay(1, QKV), 2: lambda: relay(1, OUT)},
        ),
    )
    for i in range(OUT + 1, ITEMS):
        send(1, i)
        to_sibling(1, i).start()
    out_wait(0)

    seq_send_rows(1, cols[0])
    relay_other(1, QKV)
    relay_other(1, OUT)
    moved[...] = matmul(keep[...], cols[0]).astype(BF16)
    seq_receive(1)

    def place_arrived(chip, i):
        at = pl.ds(pl.multiple_of(chip * PATCH + i * chunk, chunk), chunk)
        moved[at] = (moved[at].astype(F32) + matmul(spread[at], got[...])).astype(BF16)

    for i in range(2):
        place_arrived(other_chip, i)
        to_partner(1, i).start()
    for i in range(2):
        place_arrived(mine_chip, i)
        own(1, i).start()
        to_sibling(1, i).start()
    relay(1, UP[0])
    relay(1, UP[1])

    @pl.loop(0, slots // LANES)
    def _(i):
        at = block(i, LANES)
        both = codes[at]
        place_col = (both[:, 0:1] * BASE + both[:, 1:2]).astype(jnp.int32) - BASE
        pick[at] = chosen_cols(place_col, points)

    relay(1, DOWN[0])
    relay(1, DOWN[1])
    relay(1, 0)
    relay(1, 1)
    ready(1, 0)
    normalise(1, 0)
    ready(1, QKV)
    for chip in range(n_head // 2):
        keys_values(1, chip, 0)
    ready(1, 1)
    normalise(1, 1)
    for chip in range(n_head // 2):
        keys_values(1, chip, 1)
    for chip in range(n_head // 2):
        queries(1, chip)
    def relay_ups():
        for i in UP:
            relay_other(1, i)

    def relay_downs():
        for i in DOWN:
            relay_other(1, i)

    attend(0, n_head, {1: relay_ups, 2: relay_downs})
    for i in range(OUT, ITEMS):
        ready(1, i)
    feed_forward(1, ({}, {}))

    @pl.loop(0, points // LANES)
    def _(i):
        at = block(i, LANES)
        keep[at] = chosen_cols(code_ref[at, 3:4].astype(jnp.int32), points)

    out_wait(1)
    seq_send_rows(2, cols[1])

    @pl.loop(0, points // LANES)
    def _(i):
        at = block(i, LANES)
        spread[at] = chosen_cols(code_ref[at, 2:3].astype(jnp.int32), slots)

    for i in range(QKV):
        to_partner(1, i).wait_send()
        to_sibling(1, i).wait_send()
    moved[...] = matmul(keep[...], cols[1]).astype(BF16)
    seq_receive(2)
    final_ref[...] = (moved[...].astype(F32) + matmul(spread[...], got[...])).astype(BF16)

    for l in range(2):
        for i in range(ITEMS):
            if l == 0 or i >= QKV:
                to_partner(l, i).wait_send()
                to_sibling(l, i).wait_send()
            forward(l, i).wait_send()
            if i >= QKV:
                to_neighbour(l, i).wait_send()
                forward_other(l, i).wait_send()
    for turn in range(3):
        for step in range(1, peers):
            seq_copy(turn, step).wait_send()


def on_device(peers, n_head, x_points, hilbert_index, w_qkv, w_out, w_up, w_down):
    points, cols = x_points.shape
    near = 3 * points // 16
    cap = points // (8 * peers)
    slots = 2 * near + peers * cap
    vmem = pl.BlockSpec(memory_space=pltpu.VMEM)
    w_qkv = jnp.transpose(w_qkv, (0, 2, 1, 3))

    width = cols * n_head
    own_rows = points // n_head
    hidden = w_up.shape[1] * n_head
    layers = w_up.shape[0]
    hbm = pl.BlockSpec(memory_space=pl.ANY)
    return pl.pallas_call(
        functools.partial(program_kernel, n_head, peers, near, cap),
        out_shape=jax.ShapeDtypeStruct((points, cols), BF16),
        in_specs=[hbm] * 5 + [vmem],
        out_specs=vmem,
        scratch_shapes=[
            pltpu.VMEM((layers, PATCH, width), BF16),
            pltpu.VMEM((layers, n_head // 2, 3, width, 2 * LANES), BF16),
            pltpu.VMEM((layers, width, width), BF16),
            pltpu.VMEM((layers, hidden, width), BF16),
            pltpu.VMEM((layers, hidden, width), BF16),
            pltpu.VMEM((PATCH, width), BF16),
            pltpu.VMEM((n_head, own_rows, LANES), BF16),
            pltpu.VMEM((n_head, PATCH, LANES), BF16),
            pltpu.VMEM((n_head, PATCH, 2 * LANES), BF16),
            pltpu.VMEM((own_rows, width), BF16),
            pltpu.VMEM((own_rows, width), BF16),
            pltpu.VMEM((own_rows, width), BF16),
            pltpu.VMEM((layers, points, cols), BF16),
            pltpu.VMEM((points, cols), BF16),
            pltpu.VMEM((slots, points), BF16),
            pltpu.VMEM((points, points), BF16),
            pltpu.VMEM((points, slots), BF16),
            pltpu.VMEM((3, 2 * near, cols), BF16),
            pltpu.VMEM((3, peers, cap, cols), BF16),
            pltpu.VMEM((3, 2 * near, cols), BF16),
            pltpu.VMEM((3, peers, cap, cols), BF16),
            pltpu.VMEM((slots, cols), BF16),
            pltpu.VMEM((slots, cols), F32),
            pltpu.VMEM((256, width), F32),
            pltpu.VMEM((points, LANES), F32),
            pltpu.SemaphoreType.REGULAR((peers.bit_length() - 1,)),
            pltpu.SemaphoreType.DMA((layers, ITEMS)),
            pltpu.SemaphoreType.DMA((layers, ITEMS, 5)),
            pltpu.SemaphoreType.DMA((layers, ITEMS, 5)),
            pltpu.SemaphoreType.DMA((layers, own_rows // 256, n_head)),
            pltpu.SemaphoreType.DMA((layers, own_rows // 256, n_head)),
            pltpu.SemaphoreType.DMA((3, peers)),
            pltpu.SemaphoreType.DMA((3, peers)),
        ],
        compiler_params=pltpu.CompilerParams(
            collective_id=0, has_side_effects=True, vmem_limit_bytes=60 * 1024 * 1024
        ),
        name="point_layers",
    )(x_points, w_qkv, w_out, w_up, w_down, hilbert_index.reshape(1, points))


def solution(mesh):
    return jax.shard_map(
        functools.partial(on_device, mesh.shape["seq"], mesh.shape["head"]),
        mesh=mesh,
        in_specs=(
            P("seq", "head"),
            P("seq"),
            P(None, None, None, "head"),
            P(None, "head", None),
            P(None, "head", None),
            P(None, "head", None),
        ),
        out_specs=P("seq", "head"),
        check_vma=False,
    )
```

```python
import functools
import math

import jax
import jax.numpy as jnp
from jax import lax
from jax.experimental import pallas as pl
from jax.experimental.pallas import tpu as pltpu
from jax.sharding import PartitionSpec as P

HEAD_DIM = 32
PATCH = 1024
EPS = 1e-05
LANES = 128
BASE = 64
MESH = pl.DeviceIdType.MESH
F32 = jnp.float32
BF16 = jnp.bfloat16


def block(index, size):
    return pl.ds(pl.multiple_of(index * size, size), size)


def norm(values):
    center = values - jnp.mean(values, axis=-1, keepdims=True)
    spread = jnp.mean(center * center, axis=-1, keepdims=True)
    return (center * lax.rsqrt(spread + EPS)).astype(BF16)


def matmul(a, b):
    return jnp.dot(a, b, preferred_element_type=F32)


def matmul_nt(a, b):
    return lax.dot_general(a, b, (((1,), (1,)), ((), ())), preferred_element_type=F32)


def gelu(x):
    return 0.5 * x * (1.0 + lax.erf(x * math.sqrt(0.5)))


def chosen_rows(count, base, index_row):
    slots = lax.broadcasted_iota(jnp.int32, (count, index_row.shape[1]), 0) + base
    return (slots == index_row).astype(F32).astype(BF16)


def chosen_cols(index_col, count):
    slots = lax.broadcasted_iota(jnp.int32, (index_col.shape[0], count), 1)
    return (slots == index_col).astype(F32).astype(BF16)


CHUNKS = 4
QKV, OUT = CHUNKS, CHUNKS + 1
UP = (CHUNKS + 2, CHUNKS + 4)
DOWN = (CHUNKS + 3, CHUNKS + 5)
ITEMS = CHUNKS + 6


def program_kernel(
    n_head, peers, near, cap,
    x_ref, wqkv_ref, wout_ref, wup_ref, wdown_ref, index_ref,
    final_ref,
    rows, wqkv, wout, wup, wdown, normed, q, k, v, attended, mid_norm, result, cols, moved,
    pick, early, keep, spread, near_out, far_out, near_in, far_in, got, codes, partial, code_ref,
    met, local_sem, send_sem, recv_sem, out_send, out_recv, seq_send, seq_recv,
):
    me = lax.axis_index("head")
    seq = lax.axis_index("seq")
    sibling = me + 1 - 2 * lax.rem(me, 2)
    partner = lax.rem(me + n_head // 2, n_head)
    half = lax.rem(me, 2)
    own_rows, width = result.shape
    points = moved.shape[0]
    slots = 2 * near + peers * cap
    chunk = PATCH // CHUNKS

    barrier = pltpu.get_barrier_semaphore()
    for step in range(1, n_head):
        to = lax.rem(me + step, n_head)
        pl.semaphore_signal(barrier, inc=1, device_id={"head": to}, device_id_type=MESH)
    rounds = peers.bit_length() - 1

    def across(turn):
        return seq + 2**turn - 2 ** (turn + 1) * lax.rem(seq // 2**turn, 2)

    def greet(sem, turn):
        pl.semaphore_signal(sem, inc=1, device_id={"seq": across(turn)}, device_id_type=MESH)

    for turn in range(rounds):
        greet(barrier, turn)
    pl.semaphore_wait(barrier, n_head - 1 + rounds)

    def entered(turn):
        pl.semaphore_wait(met.at[turn], 1)
        if turn + 1 < rounds:
            greet(met.at[turn + 1], turn + 1)

    def side_of(i):
        return lax.rem(seq // 2, 2) if i in (UP[1], DOWN[1]) else lax.rem(seq, 2)

    def neighbour_of(i):
        return across(1) if i in (UP[1], DOWN[1]) else across(0)

    hidden = wup.shape[1]
    hidden_half = hidden // n_head // 2

    def source(l, i, to):
        if i < CHUNKS:
            start = pl.multiple_of((to // 2) * PATCH + i * chunk, chunk)
            return (x_ref if l == 0 else moved).at[pl.ds(start, chunk)]
        if i in (QKV, OUT):
            return (wqkv_ref if i == QKV else wout_ref).at[l]
        ref, turn = (wup_ref, UP.index(i)) if i in UP else (wdown_ref, DOWN.index(i))
        return ref.at[l, pl.ds(turn * hidden_half, hidden_half)]

    def place(l, i, owner):
        if i < CHUNKS:
            return rows.at[l, pl.ds(i * chunk, chunk), block(owner, LANES)]
        if i == QKV:
            return wqkv.at[l, owner // 2, :, :, block(lax.rem(owner, 2), LANES)]
        if i == OUT:
            return wout.at[l, block(owner, wout.shape[1] // n_head)]
        ref, turn = (wup, UP.index(i)) if i in UP else (wdown, DOWN.index(i))
        return ref.at[l, block((owner // 2 * 2 + turn) * 2 + lax.rem(owner, 2), hidden_half)]

    def part(i, ref, which):
        if i < CHUNKS:
            return ref
        if i == QKV:
            return ref.at[:, block(which, ref.shape[1] // 2)]
        return ref.at[block(which, ref.shape[0] // 2)]

    def own(l, i):
        return pltpu.make_async_copy(source(l, i, me), place(l, i, me), local_sem.at[l, i])

    def remote(l, i, way, src, dst, device):
        return pltpu.make_async_remote_copy(
            src_ref=src,
            dst_ref=dst,
            send_sem=send_sem.at[l, i, way],
            recv_sem=recv_sem.at[l, i, way],
            device_id=device,
            device_id_type=MESH,
        )

    def to_partner(l, i):
        src = part(i, source(l, i, partner), side_of(i))
        return remote(l, i, 0, src, part(i, place(l, i, me), side_of(i)), {"head": partner})

    def to_sibling(l, i):
        return remote(l, i, 1, source(l, i, sibling), place(l, i, me), {"head": sibling})

    def forward(l, i):
        ref = part(i, place(l, i, partner), side_of(i))
        return remote(l, i, 2, ref, ref, {"head": sibling})

    def to_neighbour(l, i):
        ref = part(i, place(l, i, partner), side_of(i))
        return remote(l, i, 3, ref, ref, {"seq": neighbour_of(i)})

    def forward_other(l, i):
        ref = part(i, place(l, i, partner), 1 - side_of(i))
        return remote(l, i, 4, ref, ref, {"head": sibling})

    def send(l, i):
        to_partner(l, i).start()
        own(l, i).start()

    def relay(l, i):
        to_partner(l, i).wait_recv()
        if i >= QKV:
            to_neighbour(l, i).start()
        forward(l, i).start()

    def relay_other(l, i):
        to_neighbour(l, i).wait_recv()
        forward_other(l, i).start()

    def near_ready(l, i):
        own(l, i).wait()
        to_sibling(l, i).wait_recv()

    def far_ready(l, i):
        forward(l, i).wait_recv()
        if i >= QKV:
            forward_other(l, i).wait_recv()

    def ready(l, i):
        near_ready(l, i)
        far_ready(l, i)

    def seq_copy(turn, step):
        to = lax.rem(seq + step, peers)
        back = turn == 2
        if step == 1:
            at = pl.ds(near if back else 0, near)
            src, dst = near_out.at[turn, at], near_in.at[turn, at]
        elif step == peers - 1:
            at = pl.ds(0 if back else near, near)
            src, dst = near_out.at[turn, at], near_in.at[turn, at]
        else:
            src, dst = far_out.at[turn, to], far_in.at[turn, seq]
        return pltpu.make_async_remote_copy(
            src_ref=src,
            dst_ref=dst,
            send_sem=seq_send.at[turn, step],
            recv_sem=seq_recv.at[turn, step],
            device_id={"seq": to},
            device_id_type=MESH,
        )

    def seq_send_rows(turn, found):
        for lo in range(0, 2 * near, near):
            near_out[turn, lo : lo + near] = found(lo, lo + near).astype(BF16)
            seq_copy(turn, (1 if lo == 0 else peers - 1) if turn != 2 else (peers - 1 if lo == 0 else 1)).start()
        packed = found(2 * near, slots)
        for peer in range(peers):
            far_out[turn, peer] = packed[peer * cap : (peer + 1) * cap].astype(BF16)
        for step in range(2, peers - 1):
            seq_copy(turn, step).start()

    def picked(l, piece, lo, hi):
        found = None
        for start in range(piece * 256, points, own_rows):
            at = slice(start, start + 256)
            term = matmul(pick[lo:hi, at], cols[l, at])
            found = term if found is None else found + term
        return found

    def seq_receive(turn):
        for step in range(1, peers):
            seq_copy(turn, step).wait_recv()
        for step in (0, 1, peers - 1):
            unused = lax.rem(seq + step, peers)
            far_in[turn, unused] = jnp.zeros(far_in.shape[2:], BF16)
        got[: 2 * near] = near_in[turn]
        for peer in range(peers):
            at = 2 * near + peer * cap
            got[at : at + cap] = far_in[turn, peer].astype(F32).astype(BF16)

    def normalise(l, i):
        @pl.loop(0, chunk // LANES)
        def _(j):
            at = pl.ds(pl.multiple_of(i * chunk + j * LANES, LANES), LANES)
            normed[at] = norm(rows[l, at].astype(F32))

    def keys_values(l, chip, i):
        at = pl.ds(i * chunk, chunk)
        keys = matmul(normed[at], wqkv[l, chip, 1]).astype(BF16)
        values = matmul(normed[at], wqkv[l, chip, 2]).astype(BF16)
        for part_of in range(2):
            cut = slice(part_of * LANES, (part_of + 1) * LANES)
            k[chip * 2 + part_of, at] = keys[:, cut]
            v[chip * 2 + part_of, at, :LANES] = values[:, cut]

    def queries(l, chip):
        scale = HEAD_DIM ** (-0.5) * math.log2(math.e)
        mine = pl.ds(pl.multiple_of(half * own_rows, own_rows), own_rows)
        found = (matmul(normed[mine], wqkv[l, chip, 0]) * scale).astype(BF16)
        for part_of in range(2):
            q[chip * 2 + part_of] = found[:, part_of * LANES : (part_of + 1) * LANES]

    def attend(first, count, between):
        owner = lax.broadcasted_iota(jnp.int32, (own_rows, LANES), 1) // HEAD_DIM

        @pl.loop(0, count)
        def _(step):
            for turn, action in between.items():
                pl.when(step == turn)(action)
            group = first + step
            query = q[group]

            def scores_of(head):
                return matmul_nt(jnp.where(owner == head, query, jnp.zeros_like(query)), k[group])

            total = jnp.zeros((own_rows, LANES), F32)
            norms = jnp.ones((own_rows, LANES), F32)
            scores = scores_of(0)
            for head in range(LANES // HEAD_DIM):
                following = scores_of(head + 1) if head + 1 < LANES // HEAD_DIM else None
                top = jnp.max(scores, axis=-1, keepdims=True)
                weights = jnp.exp2(scores - top).astype(BF16)
                mixed = matmul(weights, v[group])
                total = jnp.where(owner == head, mixed[:, :LANES], total)
                norms = jnp.where(owner == head, mixed[:, LANES:], norms)
                scores = following
            attended[:, block(group, LANES)] = (total / norms).astype(BF16)

    def out_copy(l, piece, step):
        to = lax.rem(me + step, n_head)
        at = pl.ds(pl.multiple_of(me * own_rows + piece * 256, 256), 256)
        return pltpu.make_async_remote_copy(
            src_ref=result.at[block(piece, 256), block(to, LANES)],
            dst_ref=cols.at[l, at],
            send_sem=out_send.at[l, piece, step],
            recv_sem=out_recv.at[l, piece, step],
            device_id={"head": to},
            device_id_type=MESH,
        )

    hidden_cols = hidden // n_head

    def feed_forward(l, between):
        for piece in range(own_rows // 256):
            at = pl.ds(piece * 256, 256)
            mine = pl.ds(pl.multiple_of(half * own_rows + piece * 256, 256), 256)
            summed = (rows[l, mine].astype(F32) + matmul(attended[at], wout[l])).astype(BF16)
            total = summed.astype(F32)
            mid_norm[at] = norm(total)
            partial[...] = total

            @pl.loop(0, n_head // 2)
            def _(j):
                for turn, action in between[piece].items():
                    pl.when(j == turn // 2)(action)
                first = block(lax.rem(me // 2 * 2 + 2 * j, n_head), hidden_cols)
                second = block(lax.rem(me // 2 * 2 + 2 * j + 1, n_head), hidden_cols)
                raised = matmul_nt(mid_norm[at], wup[l, first])
                later = matmul_nt(mid_norm[at], wup[l, second])
                lowered = matmul(gelu(raised).astype(BF16), wdown[l, first])
                partial[...] += lowered + matmul(gelu(later).astype(BF16), wdown[l, second])

            result[at] = partial[...].astype(BF16)
            for step in range(2, n_head):
                out_copy(l, piece, step).start()
            out_copy(l, piece, 1).start()
            cols[l, pl.ds(pl.multiple_of(me * own_rows + piece * 256, 256), 256)] = result[
                at, block(me, LANES)
            ]

    pieces = own_rows // 256

    def out_wait(l):
        for piece in range(pieces):
            for step in range(1, n_head):
                out_copy(l, piece, step).wait()
            if piece + 1 < pieces:
                found = picked(l, piece, 0, slots)
                early[...] = found if piece == 0 else early[...] + found

    def last_picked(l):
        return lambda lo, hi: early[lo:hi] + picked(l, pieces - 1, lo, hi)

    greet(met.at[0], 0)
    for i in range(ITEMS):
        send(0, i)
        if i <= QKV:
            to_sibling(0, i).start()
    send(1, QKV)
    send(1, OUT)

    where_to = index_ref[...]
    bounds = lax.broadcasted_iota(jnp.int32, (peers, points), 0) * points
    hot = jnp.where((where_to >= bounds) & (where_to < bounds + points), 1.0, 0.0)
    lower = lax.broadcasted_iota(jnp.int32, (LANES, LANES), 0)
    upper = lax.broadcasted_iota(jnp.int32, (LANES, LANES), 1)
    triangle = jnp.where(lower <= upper, 1.0, 0.0).astype(BF16)
    carried = jnp.zeros((peers, 1), F32)
    counts = []
    for at in range(0, points, LANES):
        piece = hot[:, at : at + LANES]
        counts.append(matmul(piece.astype(BF16), triangle) + carried)
        carried = carried + jnp.sum(piece, axis=1, keepdims=True)
    rank = jnp.sum(jnp.concatenate(counts, axis=1) * hot, axis=0, keepdims=True)
    rank = rank.astype(jnp.int32) - 1
    device_start = jnp.sum(hot * bounds.astype(F32), axis=0, keepdims=True).astype(jnp.int32)
    order = lax.broadcasted_iota(jnp.int32, (peers, points), 0).astype(F32)
    device = jnp.sum(hot * order, axis=0, keepdims=True).astype(jnp.int32)
    row = where_to - device_start
    following = lax.rem(seq + 1, peers)
    previous = lax.rem(seq + peers - 1, peers)
    slot = jnp.where(device == previous, near + rank, 2 * near + device * cap + rank)
    slot = jnp.where(device == following, rank, slot)
    slot = jnp.where(device == seq, -1, slot)
    kept = jnp.where(device == seq, row, -1)
    coded = row + BASE
    high = lax.shift_right_logical(coded, jnp.full_like(coded, BASE.bit_length() - 1))
    low = coded - high * BASE
    lane = lax.broadcasted_iota(jnp.int32, (LANES, points), 0)
    fields = jnp.where(lane == 2, slot, jnp.where(lane == 3, kept, 0))
    fields = jnp.where(lane == 0, high, jnp.where(lane == 1, low, fields))
    code_ref[...] = jnp.transpose(fields.astype(F32), (1, 0))

    @pl.loop(0, slots // LANES)
    def _(i):
        pick[block(i, LANES)] = chosen_rows(LANES, i * LANES, slot)

    for turn in range(rounds):
        entered(turn)
    seq_send_rows(0, lambda lo, hi: matmul(pick[lo:hi], code_ref[...].astype(BF16)))

    @pl.loop(0, points // LANES)
    def _(i):
        keep[block(i, LANES)] = chosen_rows(LANES, i * LANES, kept)

    relay(0, 0)
    for group in range(n_head):
        v[group, :, LANES:] = jnp.ones((PATCH, LANES), BF16)
    mine_chip = me // 2
    other_chip = partner // 2
    near_ready(0, QKV)
    for i in range(CHUNKS):
        if i + 1 < CHUNKS:
            relay(0, i + 1)
        ready(0, i)
        normalise(0, i)
        keys_values(0, mine_chip, i)
    queries(0, mine_chip)
    seq_receive(0)
    codes[...] = got[...].astype(F32)
    turned = jnp.transpose(codes[...], (1, 0))
    target = (turned[0:1] * BASE + turned[1:2]).astype(jnp.int32) - BASE

    @pl.loop(0, points // LANES)
    def _(i):
        spread[block(i, LANES)] = chosen_rows(LANES, i * LANES, target)

    relay(0, QKV)
    for i in range(OUT, ITEMS):
        to_sibling(0, i).start()
    attend(mine_chip * 2, 2, {1: lambda: relay(0, OUT)})
    relay_other(0, QKV)
    relay(0, UP[0])
    relay_other(0, OUT)

    relay(0, DOWN[0])
    far_ready(0, QKV)
    for i in range(CHUNKS):
        keys_values(0, other_chip, i)
    queries(0, other_chip)
    relay(0, UP[1])

    def relay_last():
        relay(0, DOWN[1])
        relay_other(0, UP[0])

    attend(other_chip * 2, 2, {1: relay_last})
    relay_other(0, DOWN[0])
    to_sibling(1, QKV).start()
    to_sibling(1, OUT).start()
    ready(0, OUT)
    for i in UP + DOWN:
        near_ready(0, i)

    def first_far():
        far_ready(0, UP[0])
        far_ready(0, DOWN[0])
        relay_other(0, UP[1])

    def last_far():
        relay_other(0, DOWN[1])
        far_ready(0, UP[1])
        far_ready(0, DOWN[1])

    feed_forward(
        0,
        (
            {n_head // 2: first_far, n_head - 1: last_far},
            {0: lambda: relay(1, QKV), 2: lambda: relay(1, OUT)},
        ),
    )
    for i in range(OUT + 1, ITEMS):
        send(1, i)
        to_sibling(1, i).start()
    out_wait(0)

    seq_send_rows(1, last_picked(0))
    relay_other(1, QKV)
    relay_other(1, OUT)
    moved[...] = matmul(keep[...], cols[0]).astype(BF16)
    seq_receive(1)

    def place_arrived(chip, i):
        at = pl.ds(pl.multiple_of(chip * PATCH + i * chunk, chunk), chunk)
        moved[at] = (moved[at].astype(F32) + matmul(spread[at], got[...])).astype(BF16)

    for i in range(CHUNKS):
        place_arrived(other_chip, i)
        to_partner(1, i).start()
    for i in range(CHUNKS):
        place_arrived(mine_chip, i)
        own(1, i).start()
        to_sibling(1, i).start()
    relay(1, UP[0])
    relay(1, UP[1])

    @pl.loop(0, slots // LANES)
    def _(i):
        at = block(i, LANES)
        both = codes[at]
        place_col = (both[:, 0:1] * BASE + both[:, 1:2]).astype(jnp.int32) - BASE
        pick[at] = chosen_cols(place_col, points)

    relay(1, DOWN[0])
    relay(1, DOWN[1])
    relay(1, 0)
    for i in range(CHUNKS):
        if i + 1 < CHUNKS:
            relay(1, i + 1)
        ready(1, i)
        normalise(1, i)
        if i == 0:
            ready(1, QKV)
        for chip in range(n_head // 2):
            keys_values(1, chip, i)
    for chip in range(n_head // 2):
        queries(1, chip)
    def relay_ups():
        for i in UP:
            relay_other(1, i)

    def relay_downs():
        for i in DOWN:
            relay_other(1, i)

    attend(0, n_head, {1: relay_ups, 2: relay_downs})
    for i in range(OUT, ITEMS):
        ready(1, i)
    feed_forward(1, ({}, {}))

    @pl.loop(0, points // LANES)
    def _(i):
        at = block(i, LANES)
        keep[at] = chosen_cols(code_ref[at, 3:4].astype(jnp.int32), points)

    out_wait(1)
    seq_send_rows(2, last_picked(1))

    @pl.loop(0, points // LANES)
    def _(i):
        at = block(i, LANES)
        spread[at] = chosen_cols(code_ref[at, 2:3].astype(jnp.int32), slots)

    for i in range(QKV):
        to_partner(1, i).wait_send()
        to_sibling(1, i).wait_send()
    moved[...] = matmul(keep[...], cols[1]).astype(BF16)
    seq_receive(2)
    final_ref[...] = (moved[...].astype(F32) + matmul(spread[...], got[...])).astype(BF16)

    for l in range(2):
        for i in range(ITEMS):
            if l == 0 or i >= QKV:
                to_partner(l, i).wait_send()
                to_sibling(l, i).wait_send()
            forward(l, i).wait_send()
            if i >= QKV:
                to_neighbour(l, i).wait_send()
                forward_other(l, i).wait_send()
    for turn in range(3):
        for step in range(1, peers):
            seq_copy(turn, step).wait_send()


def on_device(peers, n_head, x_points, hilbert_index, w_qkv, w_out, w_up, w_down):
    points, cols = x_points.shape
    near = 3 * points // 16
    cap = points // (8 * peers)
    slots = 2 * near + peers * cap
    vmem = pl.BlockSpec(memory_space=pltpu.VMEM)
    w_qkv = jnp.transpose(w_qkv, (0, 2, 1, 3))

    width = cols * n_head
    own_rows = points // n_head
    hidden = w_up.shape[1] * n_head
    layers = w_up.shape[0]
    hbm = pl.BlockSpec(memory_space=pl.ANY)
    return pl.pallas_call(
        functools.partial(program_kernel, n_head, peers, near, cap),
        out_shape=jax.ShapeDtypeStruct((points, cols), BF16),
        in_specs=[hbm] * 5 + [vmem],
        out_specs=vmem,
        scratch_shapes=[
            pltpu.VMEM((layers, PATCH, width), BF16),
            pltpu.VMEM((layers, n_head // 2, 3, width, 2 * LANES), BF16),
            pltpu.VMEM((layers, width, width), BF16),
            pltpu.VMEM((layers, hidden, width), BF16),
            pltpu.VMEM((layers, hidden, width), BF16),
            pltpu.VMEM((PATCH, width), BF16),
            pltpu.VMEM((n_head, own_rows, LANES), BF16),
            pltpu.VMEM((n_head, PATCH, LANES), BF16),
            pltpu.VMEM((n_head, PATCH, 2 * LANES), BF16),
            pltpu.VMEM((own_rows, width), BF16),
            pltpu.VMEM((own_rows, width), BF16),
            pltpu.VMEM((own_rows, width), BF16),
            pltpu.VMEM((layers, points, cols), BF16),
            pltpu.VMEM((points, cols), BF16),
            pltpu.VMEM((slots, points), BF16),
            pltpu.VMEM((slots, cols), F32),
            pltpu.VMEM((points, points), BF16),
            pltpu.VMEM((points, slots), BF16),
            pltpu.VMEM((3, 2 * near, cols), BF16),
            pltpu.VMEM((3, peers, cap, cols), BF16),
            pltpu.VMEM((3, 2 * near, cols), BF16),
            pltpu.VMEM((3, peers, cap, cols), BF16),
            pltpu.VMEM((slots, cols), BF16),
            pltpu.VMEM((slots, cols), F32),
            pltpu.VMEM((256, width), F32),
            pltpu.VMEM((points, LANES), F32),
            pltpu.SemaphoreType.REGULAR((peers.bit_length() - 1,)),
            pltpu.SemaphoreType.DMA((layers, ITEMS)),
            pltpu.SemaphoreType.DMA((layers, ITEMS, 5)),
            pltpu.SemaphoreType.DMA((layers, ITEMS, 5)),
            pltpu.SemaphoreType.DMA((layers, own_rows // 256, n_head)),
            pltpu.SemaphoreType.DMA((layers, own_rows // 256, n_head)),
            pltpu.SemaphoreType.DMA((3, peers)),
            pltpu.SemaphoreType.DMA((3, peers)),
        ],
        compiler_params=pltpu.CompilerParams(
            collective_id=0, has_side_effects=True, vmem_limit_bytes=60 * 1024 * 1024
        ),
        name="point_layers",
    )(x_points, w_qkv, w_out, w_up, w_down, hilbert_index.reshape(1, points))


def solution(mesh):
    return jax.shard_map(
        functools.partial(on_device, mesh.shape["seq"], mesh.shape["head"]),
        mesh=mesh,
        in_specs=(
            P("seq", "head"),
            P("seq"),
            P(None, None, None, "head"),
            P(None, "head", None),
            P(None, "head", None),
            P(None, "head", None),
        ),
        out_specs=P("seq", "head"),
        check_vma=False,
    )
```
